256 devices in a mesh: chain: 16 (over z, y_lo), cand: 16 (over y_hi, x, core).
Axes of the slice: x: 4, y: 4 (y_hi: 2, y_lo: 2; y = y_hi * 2 + y_lo), z: 8, core: 2. Of those that a mesh axis runs over, the one named last changes fastest.
Arguments:
- archive_inputs: float32 [32, 3072], P(None, 'chain'), may hold values from -6 to 6
- candidate_inputs: float32 [32, 2048], P(None, 'cand'), may hold values from -6 to 6
- lengthscales: float32 [32], replicated, may hold values from 3 to 10
- factor: float32 [3072, 3072], P('chain'), as said below
Outputs:
- whitened: float32 [3072, 2048], P('chain', 'cand')
- corrected_cov: float32 [2048, 2048], P('chain', 'cand')
The draws below stay inside these ranges and needn't reach their ends.
Inputs may be any that keep to these rules, and one draw needn't show every extreme that they name: factor is lower triangular (zeros above the diagonal); its diagonal lies between 0.2 * sqrt(3072) and 0.5 * sqrt(3072).
All inputs are finite; a program needn't handle non-finite values.
Results may differ from the reference program's by a relative error of at most 0.000076.
Values sent between devices are 32-bit elements; how exact they have to be, the bound alone decides.
No kernel may reach another device: no remote copies, remote signals or barrier semaphores. Data moves between devices by JAX's collectives and lax.ppermute only.
A program may use at most 64 MiB of HBM per device.

```python
import math
import jax
import jax.numpy as jnp
from jax import lax

DIMS = 32
ROWS_DEV = 192
CAND_DEV = 128
ARCH = 3072
CANDS = 2048


def draw_factor(key, part):
    first_key, second_key = jax.random.split(jax.random.fold_in(key, 7))
    scale_root = jnp.sqrt(jnp.float32(ARCH))
    diagonal = scale_root * jnp.exp(jax.random.uniform(first_key, (ARCH,), jnp.float32, jnp.log(0.2), jnp.log(0.5)))
    spread = jnp.clip(0.12 * jax.random.normal(second_key, (ARCH, ARCH), jnp.float32), -0.6, 0.6)
    lower = jnp.tril(spread, -1) + jnp.diag(diagonal)
    return lower.astype(jnp.float32)


def block_levels(stream_key, extent, shards, least, top_value):
    level = 1.0
    for position, shards_of in shards:
        steps = jax.random.uniform(jax.random.fold_in(jax.random.fold_in(stream_key, 6), position), (shards_of,), jnp.float32, least / len(shards), top_value / len(shards))
        level = level * jnp.repeat(jnp.exp(steps), extent[position] // shards_of).reshape((-1,) + (1,) * (len(extent) - 1 - position))
    return level


def noise(own_key, extent, width, bound, shards=(), dtype=jnp.bfloat16):
    loudness = block_levels(own_key, extent, shards, -0.22, 0.18) if shards else 1.0
    array = jax.random.normal(own_key, extent, jnp.float32) * width * loudness
    return jnp.minimum(jnp.maximum(array, -bound), bound).astype(dtype)


def setup_inputs(seed: int = 0) -> dict:
    splits = jax.random.split(jax.random.key(seed), 5)
    return {
        "archive_inputs": noise(splits[0], (DIMS, ARCH), 1.0, 6.0, ((1, 16),), jnp.float32),
        "candidate_inputs": noise(splits[1], (DIMS, CANDS), 1.0, 6.0, ((1, 16),), jnp.float32),
        "lengthscales": jnp.clip(jnp.exp(jax.random.uniform(splits[2], (DIMS,), jnp.float32, math.log(3.0), math.log(10.0))), 3.0, 10.0),
        "factor": draw_factor(jax.random.fold_in(splits[4], 71), 0),
    }


def matern(first_set, second_set):
    differ = first_set[:, :, None] - second_set[:, None, :]
    radius = jnp.sqrt(5.0 * lax.optimization_barrier(jnp.sum(differ * differ, axis=0)))
    return (1.0 + radius + radius * radius / 3.0) * jnp.exp(-radius)

def reference(archive_inputs, candidate_inputs, lengthscales, factor):
    scaling = 1.0 / lengthscales
    scaled_archive = archive_inputs * scaling[:, None]
    scaled_candidates = candidate_inputs * scaling[:, None]

    def against(row_batch):
        return matern(row_batch, scaled_candidates)
    archive_blocks = scaled_archive.reshape(DIMS, ARCH // ROWS_DEV, ROWS_DEV).transpose(1, 0, 2)
    cross = lax.map(against, archive_blocks).reshape(ARCH, CANDS)
    whitened = jax.scipy.linalg.solve_triangular(factor, cross, lower=True)
    candidate_blocks = scaled_candidates.reshape(DIMS, CANDS // CAND_DEV, CAND_DEV).transpose(1, 0, 2)
    prior_cov = lax.map(against, candidate_blocks).reshape(CANDS, CANDS)
    product = jnp.dot(whitened.T, whitened, precision=lax.Precision.HIGHEST)
    return (whitened, prior_cov - product)
```

```python
import jax
import jax.numpy as jnp
from jax import lax
from jax.experimental import pallas as pl
from jax.experimental.pallas import tpu as pltpu
from jax.sharding import PartitionSpec as P

HIGH = lax.Precision.HIGHEST
BASE = 32


def matern(first_set, second_set):
    differ = first_set[:, :, None] - second_set[:, None, :]
    radius = jnp.sqrt(5.0 * jnp.sum(differ * differ, axis=0))
    return (1.0 + radius + radius * radius / 3.0) * jnp.exp(-radius)


def mm(a, b):
    return jnp.dot(a, b, precision=HIGH, preferred_element_type=jnp.float32)


def invert_kernel(l_ref, d_ref):
    size = l_ref.shape[0]
    count = size // BASE
    rows = lax.broadcasted_iota(jnp.int32, (BASE, BASE), 0)
    cols = lax.broadcasted_iota(jnp.int32, (BASE, BASE), 1)
    strict, solved = [], []
    for k in range(count):
        block = l_ref[k * BASE : (k + 1) * BASE, k * BASE : (k + 1) * BASE]
        diag = jnp.sum(jnp.where(rows == cols, block, 0.0), axis=1, keepdims=True)
        inv = 1.0 / diag
        strict.append(jnp.where(rows > cols, block * inv, 0.0))
        solved.append(jnp.where(rows == cols, inv, 0.0))
    for r in range(BASE - 1):
        for k in range(count):
            solved[k] = solved[k] - strict[k][:, r : r + 1] * solved[k][r : r + 1, :]
    d_ref[...] = jnp.zeros_like(d_ref)
    for k in range(count):
        d_ref[k * BASE : (k + 1) * BASE, k * BASE : (k + 1) * BASE] = solved[k]
    for k in range(0, count - 1, 2):
        a, b, c = k * BASE, (k + 1) * BASE, (k + 2) * BASE
        d_ref[b:c, a:b] = -mm(solved[k + 1], mm(l_ref[b:c, a:b], solved[k]))
    low = 2 * BASE
    while low < size:
        high = low + 2 * BASE
        d_ref[low:high, 0:low] = -mm(
            d_ref[low:high, low:high], mm(l_ref[low:high, 0:low], d_ref[0:low, 0:low])
        )
        low = high


def invert(block):
    return pl.pallas_call(
        invert_kernel, out_shape=jax.ShapeDtypeStruct(block.shape, jnp.float32)
    )(block)


def couple_kernel(d_ref, l_ref, g_ref):
    height = d_ref.shape[0]
    count = l_ref.shape[1] // height
    g_ref[0] = jnp.zeros((height, height), jnp.float32)
    inverse = d_ref[...]
    for k in range(count):
        g_ref[k + 1] = mm(inverse, l_ref[:, k * height : (k + 1) * height])


def couple(inverse, factor):
    height = inverse.shape[0]
    count = factor.shape[1] // height
    return pl.pallas_call(
        couple_kernel,
        out_shape=jax.ShapeDtypeStruct((count + 1, height, height), jnp.float32),
    )(inverse, factor)


def spread(value, axis, size, groups=None):
    copies = jnp.broadcast_to(value[None], (size,) + value.shape)
    return lax.all_to_all(copies, axis, 0, 0, axis_index_groups=groups, tiled=True)


def shards(archive_inputs, candidate_inputs, lengthscales, factor):
    height = factor.shape[0]
    chain = lax.axis_size("chain")
    cand = lax.axis_size("cand")
    quad = 4
    quads = chain // quad
    position = lax.axis_index("chain")
    scaling = 1.0 / lengthscales
    scaled_archive = archive_inputs * scaling[:, None]
    scaled_candidates = candidate_inputs * scaling[:, None]

    swap = [(a * cand + b, b * cand + a) for a in range(chain) for b in range(cand)]
    chosen = lax.ppermute(candidate_inputs, ("chain", "cand"), swap)
    own = lax.dynamic_slice_in_dim(factor, position * height, height, 1)
    inverse = invert(own)
    blocks = couple(inverse, factor)
    rows = mm(inverse, matern(scaled_archive, scaled_candidates))

    for t in range(chain - 1):
        near = [(t - k, t + 1 + k) for k in range(chain) if t - k >= 0 and t + 1 + k < chain]
        far = [(t - k, t + 2 + k) for k in range(chain) if t - k >= 0 and t + 2 + k < chain]
        first = lax.ppermute(rows, "chain", near)
        index = 2 * t + 2 - position
        step = mm(lax.dynamic_index_in_dim(blocks, index, 0, keepdims=False), first)
        if far:
            second = lax.ppermute(rows, "chain", far)
            step = step + mm(lax.dynamic_index_in_dim(blocks, index + 1, 0, keepdims=False), second)
        rows = rows - step

    turn = [
        ((quad * g + j) * cand + quad * m + i, (quad * g + i) * cand + quad * j + m)
        for g in range(quads)
        for i in range(quad)
        for j in range(quad)
        for m in range(cand // quad)
    ]
    turned = lax.ppermute(rows, ("chain", "cand"), turn)
    inside = [[quad * g + i for i in range(quad)] for g in range(quads)]
    across = [[quad * g + i for g in range(quads)] for i in range(quad)]
    mine = spread(rows, "chain", quad, inside)
    others = spread(turned, "cand", cand)
    width = rows.shape[1]
    others = others.reshape(quad, cand // quad, height, width)
    shares = jnp.einsum(
        "jmra,jrb->mab", others, mine, precision=HIGH, preferred_element_type=jnp.float32
    )
    shared = lax.all_to_all(shares, "chain", 0, 0, axis_index_groups=across, tiled=True).sum(axis=0)
    prior_cov = matern(chosen * scaling[:, None], scaled_candidates)
    return (rows, prior_cov - shared)


def solution(mesh):
    return jax.shard_map(
        shards,
        mesh=mesh,
        in_specs=(P(None, "chain"), P(None, "cand"), P(), P("chain", None)),
        out_specs=(P("chain", "cand"), P("chain", "cand")),
        check_vma=False,
    )
```

```python
import jax
import jax.numpy as jnp
from jax import lax
from jax.experimental import pallas as pl
from jax.experimental.pallas import tpu as pltpu
from jax.sharding import PartitionSpec as P

HIGH = lax.Precision.HIGHEST
BASE = 32
QUAD = 4


def matern(first_set, second_set):
    differ = first_set[:, :, None] - second_set[:, None, :]
    radius = jnp.sqrt(5.0 * jnp.sum(differ * differ, axis=0))
    return (1.0 + radius + radius * radius / 3.0) * jnp.exp(-radius)


def mm(a, b):
    return jnp.dot(a, b, precision=HIGH, preferred_element_type=jnp.float32)


def invert_into(l_ref, d_ref):
    size = l_ref.shape[0]
    count = size // BASE
    rows = lax.broadcasted_iota(jnp.int32, (BASE, BASE), 0)
    cols = lax.broadcasted_iota(jnp.int32, (BASE, BASE), 1)
    strict, solved = [], []
    for k in range(count):
        block = l_ref[k * BASE : (k + 1) * BASE, k * BASE : (k + 1) * BASE]
        diag = jnp.sum(jnp.where(rows == cols, block, 0.0), axis=1, keepdims=True)
        inv = 1.0 / diag
        strict.append(jnp.where(rows > cols, block * inv, 0.0))
        solved.append(jnp.where(rows == cols, inv, 0.0))
    for r in range(BASE - 1):
        for k in range(count):
            solved[k] = solved[k] - strict[k][:, r : r + 1] * solved[k][r : r + 1, :]
    d_ref[...] = jnp.zeros_like(d_ref)
    for k in range(count):
        d_ref[k * BASE : (k + 1) * BASE, k * BASE : (k + 1) * BASE] = solved[k]
    for k in range(0, count - 1, 2):
        a, b, c = k * BASE, (k + 1) * BASE, (k + 2) * BASE
        d_ref[b:c, a:b] = -mm(solved[k + 1], mm(l_ref[b:c, a:b], solved[k]))
    low = 2 * BASE
    while low < size:
        high = low + 2 * BASE
        d_ref[low:high, 0:low] = -mm(
            d_ref[low:high, low:high], mm(l_ref[low:high, 0:low], d_ref[0:low, 0:low])
        )
        low = high


def first_kernel(where_ref, near_ref, last_ref, cross_ref, out_ref, d_ref, l_ref):
    height, width = cross_ref.shape
    member = where_ref[1]
    own = near_ref[:, 0:height]
    for k in range(1, QUAD):
        own = jnp.where(member == k, near_ref[:, k * height : (k + 1) * height], own)
    l_ref[...] = own
    invert_into(l_ref, d_ref)
    inverse = d_ref[...]
    inner = (QUAD - 1) * height
    column = lax.broadcasted_iota(jnp.int32, (height, inner), 1)
    scaled = mm(inverse, near_ref[:, 0:inner])
    scaled = jnp.where(column < member * height, scaled, 0.0)
    panel = mm(inverse, cross_ref[...])
    before = mm(inverse, last_ref[...])
    for j in range(QUAD):
        out_ref[j, :, 0:width] = panel
        out_ref[j, :, width : width + inner] = scaled
        out_ref[j, :, width + inner :] = before[:, j * height : (j + 1) * height]


def first(where, factor, cross):
    height, width = cross.shape
    span = QUAD * height
    return pl.pallas_call(
        first_kernel,
        grid_spec=pltpu.PrefetchScalarGridSpec(
            num_scalar_prefetch=1,
            grid=(1,),
            in_specs=[
                pl.BlockSpec((height, span), lambda _, s: (0, s[0])),
                pl.BlockSpec((height, span), lambda _, s: (0, jnp.maximum(s[0] - 1, 0))),
                pl.BlockSpec((height, width), lambda _, s: (0, 0)),
            ],
            out_specs=[
                pl.BlockSpec((QUAD, height, width + span), lambda _, s: (0, 0, 0)),
                pl.BlockSpec((height, height), lambda _, s: (0, 0)),
            ],
            scratch_shapes=[pltpu.VMEM((height, height), jnp.float32)],
        ),
        out_shape=[
            jax.ShapeDtypeStruct((QUAD, height, width + span), jnp.float32),
            jax.ShapeDtypeStruct((height, height), jnp.float32),
        ],
    )(where, factor, factor, cross)


def older_kernel(where_ref, d_ref, two_ref, three_ref, out_ref):
    height = d_ref.shape[0]
    inverse = d_ref[...]
    two = mm(inverse, two_ref[...])
    three = mm(inverse, three_ref[...])
    for j in range(QUAD):
        out_ref[j, :, 0:height] = two[:, j * height : (j + 1) * height]
        out_ref[j, :, height:] = three[:, j * height : (j + 1) * height]


def older(where, inverse, factor):
    height = inverse.shape[0]
    span = QUAD * height
    return pl.pallas_call(
        older_kernel,
        grid_spec=pltpu.PrefetchScalarGridSpec(
            num_scalar_prefetch=1,
            grid=(1,),
            in_specs=[
                pl.BlockSpec((height, height), lambda _, s: (0, 0)),
                pl.BlockSpec((height, span), lambda _, s: (0, jnp.maximum(s[0] - 2, 0))),
                pl.BlockSpec((height, span), lambda _, s: (0, jnp.maximum(s[0] - 3, 0))),
            ],
            out_specs=pl.BlockSpec((QUAD, height, 2 * height), lambda _, s: (0, 0, 0)),
        ),
        out_shape=jax.ShapeDtypeStruct((QUAD, height, 2 * height), jnp.float32),
    )(where, inverse, factor, factor)


def join_kernel(where_ref, got_ref, base_ref, last_ref):
    height, width = base_ref.shape
    inner = (QUAD - 1) * height
    member = where_ref[1]
    base = got_ref[0, :, 0:width]
    panels, lasts = [base], [got_ref[0, :, width + inner :]]
    last_ref[0:height, :] = lasts[0]
    for i in range(1, QUAD):
        scaled = got_ref[i, :, width : width + i * height]
        panel = got_ref[i, :, 0:width] - mm(scaled, jnp.concatenate(panels, axis=0))
        last = got_ref[i, :, width + inner :] - mm(scaled, last_ref[0 : i * height, :])
        panels.append(panel)
        last_ref[i * height : (i + 1) * height, :] = last
        base = jnp.where(member == i, panel, base)
    base_ref[...] = base


def join(where, got, width):
    height = got.shape[1]
    return pl.pallas_call(
        join_kernel,
        grid_spec=pltpu.PrefetchScalarGridSpec(
            num_scalar_prefetch=1,
            grid=(1,),
            in_specs=[pl.BlockSpec(got.shape, lambda _, s: (0, 0, 0))],
            out_specs=[
                pl.BlockSpec((height, width), lambda _, s: (0, 0)),
                pl.BlockSpec((QUAD * height, height), lambda _, s: (0, 0)),
            ],
        ),
        out_shape=[
            jax.ShapeDtypeStruct((height, width), jnp.float32),
            jax.ShapeDtypeStruct((QUAD * height, height), jnp.float32),
        ],
    )(where, got)


def join_older_kernel(got_ref, more_ref, out_ref):
    height = got_ref.shape[1]
    width = got_ref.shape[2] - QUAD * height
    out_ref[0:height, :] = more_ref[0]
    for i in range(1, QUAD):
        scaled = got_ref[i, :, width : width + i * height]
        out_ref[i * height : (i + 1) * height, :] = more_ref[i] - mm(scaled, out_ref[0 : i * height, :])


def join_older(got, more):
    height = got.shape[1]
    return pl.pallas_call(
        join_older_kernel,
        out_shape=jax.ShapeDtypeStruct((QUAD * height, 2 * height), jnp.float32),
    )(got, more)


def shards(archive_inputs, candidate_inputs, lengthscales, factor):
    height = factor.shape[0]
    width = candidate_inputs.shape[1]
    chain = lax.axis_size("chain")
    cand = lax.axis_size("cand")
    quads = chain // QUAD
    position = lax.axis_index("chain")
    group = position // QUAD
    where = jnp.stack([group, position % QUAD]).astype(jnp.int32)
    inside = [[QUAD * g + i for i in range(QUAD)] for g in range(quads)]
    across = [[QUAD * g + i for g in range(quads)] for i in range(QUAD)]
    scaling = 1.0 / lengthscales
    scaled_archive = archive_inputs * scaling[:, None]
    scaled_candidates = candidate_inputs * scaling[:, None]

    swap = [(a * cand + b, b * cand + a) for a in range(chain) for b in range(cand)]
    chosen = lax.ppermute(candidate_inputs, ("chain", "cand"), swap)
    sent, inverse = first(where, factor, matern(scaled_archive, scaled_candidates))
    got = lax.all_to_all(sent, "chain", 0, 0, axis_index_groups=inside, tiled=True)
    more = lax.all_to_all(
        older(where, inverse, factor), "chain", 0, 0, axis_index_groups=inside, tiled=True
    )
    base, last = join(where, got, width)
    earlier = join_older(got, more)
    two, three = earlier[:, 0:height], earlier[:, height:]
    mixed = jnp.where(group == 3, three, last)

    def shift(value, *hops):
        pairs = [(QUAD * a + i, QUAD * b + i) for a, b in hops for i in range(QUAD)]
        return lax.ppermute(value, "chain", pairs)

    def settle(total):
        parts = total.reshape(QUAD, height, width)
        parts = lax.all_to_all(parts, "chain", 0, 0, axis_index_groups=inside, tiled=True)
        return base - parts.sum(axis=0)

    rows = base
    total = mm(last, shift(rows, (0, 1)))
    ahead = shift(rows, (0, 2))
    rows = settle(total)
    total = total + mm(two, ahead) + mm(mixed, shift(rows, (1, 2), (0, 3)))
    ahead = shift(rows, (1, 3))
    rows = settle(total)
    total = total + mm(two, ahead) + mm(last, shift(rows, (2, 3)))
    rows = settle(total)

    turn = [
        ((QUAD * g + (i ^ j)) * cand + QUAD * m + i, (QUAD * g + i) * cand + QUAD * j + m)
        for g in range(quads)
        for i in range(QUAD)
        for j in range(QUAD)
        for m in range(cand // QUAD)
    ]
    turned = lax.ppermute(rows, ("chain", "cand"), turn)
    mine = [rows]
    for r in range(1, QUAD):
        pairs = [(QUAD * g + i, QUAD * g + (i ^ r)) for g in range(quads) for i in range(QUAD)]
        mine.append(lax.ppermute(rows, "chain", pairs))
    copies = jnp.broadcast_to(turned[None], (cand,) + turned.shape)
    others = lax.all_to_all(copies, "cand", 0, 0, tiled=True)
    others = others.reshape(QUAD, cand // QUAD, height, width)
    shares = jnp.einsum(
        "jmra,jrb->mab", others, jnp.stack(mine), precision=HIGH, preferred_element_type=jnp.float32
    )
    shared = lax.all_to_all(shares, "chain", 0, 0, axis_index_groups=across, tiled=True).sum(axis=0)
    prior_cov = matern(chosen * scaling[:, None], scaled_candidates)
    return (rows, prior_cov - shared)


def solution(mesh):
    return jax.shard_map(
        shards,
        mesh=mesh,
        in_specs=(P(None, "chain"), P(None, "cand"), P(), P("chain", None)),
        out_specs=(P("chain", "cand"), P("chain", "cand")),
        check_vma=False,
    )
```

```python
import jax
import jax.numpy as jnp
from jax import lax
from jax.experimental import pallas as pl
from jax.experimental.pallas import tpu as pltpu
from jax.sharding import PartitionSpec as P

HIGH = lax.Precision.HIGHEST
BASE = 32
QUAD = 4


def matern(first_set, second_set):
    differ = first_set[:, :, None] - second_set[:, None, :]
    radius = jnp.sqrt(5.0 * jnp.sum(differ * differ, axis=0))
    return (1.0 + radius + radius * radius / 3.0) * jnp.exp(-radius)


def mm(a, b):
    return jnp.dot(a, b, precision=HIGH, preferred_element_type=jnp.float32)


def invert_into(l_ref, d_ref):
    size = l_ref.shape[0]
    count = size // BASE
    rows = lax.broadcasted_iota(jnp.int32, (BASE, BASE), 0)
    cols = lax.broadcasted_iota(jnp.int32, (BASE, BASE), 1)
    strict, solved = [], []
    for k in range(count):
        block = l_ref[k * BASE : (k + 1) * BASE, k * BASE : (k + 1) * BASE]
        diag = jnp.sum(jnp.where(rows == cols, block, 0.0), axis=1, keepdims=True)
        inv = 1.0 / diag
        strict.append(jnp.where(rows > cols, block * inv, 0.0))
        solved.append(jnp.where(rows == cols, inv, 0.0))
    for r in range(BASE - 1):
        for k in range(count):
            solved[k] = solved[k] - strict[k][:, r : r + 1] * solved[k][r : r + 1, :]
    d_ref[...] = jnp.zeros_like(d_ref)
    for k in range(count):
        d_ref[k * BASE : (k + 1) * BASE, k * BASE : (k + 1) * BASE] = solved[k]
    for k in range(0, count - 1, 2):
        a, b, c = k * BASE, (k + 1) * BASE, (k + 2) * BASE
        d_ref[b:c, a:b] = -mm(solved[k + 1], mm(l_ref[b:c, a:b], solved[k]))
    low = 2 * BASE
    while low < size:
        high = low + 2 * BASE
        d_ref[low:high, 0:low] = -mm(
            d_ref[low:high, low:high], mm(l_ref[low:high, 0:low], d_ref[0:low, 0:low])
        )
        low = high


def unpack(panel):
    half = panel.shape[1] // 2
    return jnp.concatenate([panel[:, 0:half], panel[:, half:]], axis=0)


def pack(tall):
    height = tall.shape[0] // 2
    return jnp.concatenate([tall[0:height], tall[height:]], axis=1)


def first_kernel(side_ref, own_ref, other_ref, cross_ref, d_ref, x_ref, e_ref, o_ref, i_ref):
    height = own_ref.shape[0]
    even = side_ref[0] == 0
    e_ref[...] = jnp.where(even, own_ref[:, 0:height], other_ref[:, 0:height])
    o_ref[...] = jnp.where(even, other_ref[:, height:], own_ref[:, height:])
    couple = jnp.where(even, other_ref[:, 0:height], own_ref[:, 0:height])
    d_ref[0:height, height:] = jnp.zeros((height, height), jnp.float32)
    invert_into(e_ref, i_ref)
    upper = i_ref[...]
    d_ref[0:height, 0:height] = upper
    invert_into(o_ref, e_ref)
    lower = e_ref[...]
    d_ref[height:, height:] = lower
    d_ref[height:, 0:height] = -mm(lower, mm(couple, upper))
    x_ref[...] = pack(mm(d_ref[...], unpack(cross_ref[...])))


def first(side, own, other, cross):
    height = own.shape[0]
    square = pltpu.VMEM((height, height), jnp.float32)
    return pl.pallas_call(
        first_kernel,
        in_specs=[pl.BlockSpec(memory_space=pltpu.SMEM)] + [pl.BlockSpec(memory_space=pltpu.VMEM)] * 3,
        out_shape=[
            jax.ShapeDtypeStruct((2 * height, 2 * height), jnp.float32),
            jax.ShapeDtypeStruct(cross.shape, jnp.float32),
        ],
        scratch_shapes=[square, square, square],
    )(side, own, other, cross)


def step_kernel(pick_ref, one_ref, two_ref, d_ref, rest_ref, near_ref, far_ref, left_ref, x_ref):
    near, far = near_ref[...], far_ref[...]
    swap = pick_ref[1] == 1
    lead = jnp.where(swap, near, far)
    tail = jnp.where(swap, far, near)
    panels = jnp.concatenate([unpack(lead), unpack(tail)], axis=0)

    rows = jnp.where(pick_ref[0] == 0, one_ref[...], two_ref[...])
    left = unpack(rest_ref[...]) - mm(rows, panels)
    left_ref[...] = pack(left)
    x_ref[...] = pack(mm(d_ref[...], left))


def step(pick, one, two, inverse, rest, near, far):
    shape = jax.ShapeDtypeStruct(rest.shape, jnp.float32)
    return pl.pallas_call(
        step_kernel,
        in_specs=[pl.BlockSpec(memory_space=pltpu.SMEM)] + [pl.BlockSpec(memory_space=pltpu.VMEM)] * 6,
        out_shape=[shape, shape],
    )(pick, one, two, inverse, rest, near, far)


def shards(archive_inputs, candidate_inputs, lengthscales, factor):
    height = factor.shape[0]
    width = candidate_inputs.shape[1]
    chain = lax.axis_size("chain")
    cand = lax.axis_size("cand")
    quads = chain // QUAD
    position = lax.axis_index("chain")
    inside = [[QUAD * g + i for i in range(QUAD)] for g in range(quads)]
    across = [[QUAD * g + i for g in range(quads)] for i in range(QUAD)]
    layers = chain // 2
    layer, side = position // 2, position % 2
    odd = layer % 2
    side_word = jnp.full((1,), side, jnp.int32)
    pair_all = [(p, p ^ 1) for p in range(chain)]
    scaling = 1.0 / lengthscales
    scaled_archive = archive_inputs * scaling[:, None]
    scaled_candidates = candidate_inputs * scaling[:, None]

    def halves(own, other):
        half = width // 2
        even = jnp.concatenate([own[:, :half], other[:, :half]], axis=1)
        return jnp.where(side == 0, even, jnp.concatenate([other[:, half:], own[:, half:]], axis=1))

    own_diagonal = lax.dynamic_slice_in_dim(factor, layer * 2 * height, 2 * height, 1)
    other_diagonal = lax.ppermute(own_diagonal, "chain", pair_all)
    cross = matern(scaled_archive, scaled_candidates)
    rest = halves(cross, lax.ppermute(cross, "chain", pair_all))

    slabs = []
    for s in range(layers // 2):
        start = jnp.maximum(2 * s - odd, 0) * 2 * height
        mine = lax.dynamic_slice_in_dim(factor, start, 4 * height, 1)
        pairs = [(p, p ^ 1) for p in range(chain) if p // 2 >= 2 * s + 1]
        yours = lax.ppermute(mine, "chain", pairs)
        upper = jnp.where(side == 0, mine, yours)
        lower = jnp.where(side == 0, yours, mine)
        slabs.append(jnp.concatenate([upper, lower], axis=0))

    def hop(value, pairs):
        return lax.ppermute(value, "chain", [(2 * a + i, 2 * b + i) for a, b in pairs for i in range(2)])

    inverse, solved = first(side_word, own_diagonal, other_diagonal, rest)
    far = jnp.zeros_like(rest)
    for t in range(layers - 1):
        near = hop(solved, [(t - k, t + 1 + k) for k in range(layers) if t - k >= 0 and t + 1 + k < layers])
        pairs = [(t - k, t + 2 + k) for k in range(layers) if t - k >= 0 and t + 2 + k < layers]
        ahead = hop(solved, pairs) if pairs else None
        users = sorted({t - z // 2 for z in range(t + 1, min(2 * t + 1, layers - 1) + 1)})
        turn_of = t - layer // 2
        choice = (turn_of == users[-1]).astype(jnp.int32) if len(users) > 1 else jnp.int32(0)
        flip = jnp.logical_and(turn_of == 0, odd == 1).astype(jnp.int32)
        pick = jnp.stack([choice, flip])
        rest, solved = step(pick, slabs[users[0]], slabs[users[-1]], inverse, rest, near, far)
        far = ahead
    rows = halves(solved, lax.ppermute(solved, "chain", pair_all))
    swap = [(a * cand + b, b * cand + a) for a in range(chain) for b in range(cand)]
    chosen = lax.ppermute(candidate_inputs, ("chain", "cand"), swap)

    turn = [
        ((QUAD * g + (i ^ j)) * cand + QUAD * m + i, (QUAD * g + i) * cand + QUAD * j + m)
        for g in range(quads)
        for i in range(QUAD)
        for j in range(QUAD)
        for m in range(cand // QUAD)
    ]
    turned = lax.ppermute(rows, ("chain", "cand"), turn)
    mine = [rows]
    for r in range(1, QUAD):
        pairs = [(QUAD * g + i, QUAD * g + (i ^ r)) for g in range(quads) for i in range(QUAD)]
        mine.append(lax.ppermute(rows, "chain", pairs))
    copies = jnp.broadcast_to(turned[None], (cand,) + turned.shape)
    others = lax.all_to_all(copies, "cand", 0, 0, tiled=True)
    others = others.reshape(QUAD, cand // QUAD, height, width)
    shares = jnp.einsum(
        "jmra,jrb->mab", others, jnp.stack(mine), precision=HIGH, preferred_element_type=jnp.float32
    )
    shared = lax.all_to_all(shares, "chain", 0, 0, axis_index_groups=across, tiled=True).sum(axis=0)
    prior_cov = matern(chosen * scaling[:, None], scaled_candidates)
    return (rows, prior_cov - shared)


def solution(mesh):
    return jax.shard_map(
        shards,
        mesh=mesh,
        in_specs=(P(None, "chain"), P(None, "cand"), P(), P("chain", None)),
        out_specs=(P("chain", "cand"), P("chain", "cand")),
        check_vma=False,
    )
```

```python
import jax
import jax.numpy as jnp
from jax import lax
from jax.experimental import pallas as pl
from jax.experimental.pallas import tpu as pltpu
from jax.sharding import PartitionSpec as P

HIGH = lax.Precision.HIGHEST
BASE = 32
QUAD = 4


def matern(first_set, second_set):
    differ = first_set[:, :, None] - second_set[:, None, :]
    radius = jnp.sqrt(5.0 * jnp.sum(differ * differ, axis=0))
    return (1.0 + radius + radius * radius / 3.0) * jnp.exp(-radius)


def mm(a, b):
    return jnp.dot(a, b, precision=HIGH, preferred_element_type=jnp.float32)


def invert_into(l_ref, d_ref):
    size = l_ref.shape[0]
    count = size // BASE
    rows = lax.broadcasted_iota(jnp.int32, (BASE, BASE), 0)
    cols = lax.broadcasted_iota(jnp.int32, (BASE, BASE), 1)
    strict, solved = [], []
    for k in range(count):
        block = l_ref[k * BASE : (k + 1) * BASE, k * BASE : (k + 1) * BASE]
        diag = jnp.sum(jnp.where(rows == cols, block, 0.0), axis=1, keepdims=True)
        inv = 1.0 / diag
        strict.append(jnp.where(rows > cols, block * inv, 0.0))
        solved.append(jnp.where(rows == cols, inv, 0.0))
    for r in range(BASE - 1):
        for k in range(count):
            solved[k] = solved[k] - strict[k][:, r : r + 1] * solved[k][r : r + 1, :]
    d_ref[...] = jnp.zeros_like(d_ref)
    for k in range(count):
        d_ref[k * BASE : (k + 1) * BASE, k * BASE : (k + 1) * BASE] = solved[k]
    for k in range(0, count - 1, 2):
        a, b, c = k * BASE, (k + 1) * BASE, (k + 2) * BASE
        d_ref[b:c, a:b] = -mm(solved[k + 1], mm(l_ref[b:c, a:b], solved[k]))
    low = 2 * BASE
    while low < size:
        high = low + 2 * BASE
        d_ref[low:high, 0:low] = -mm(
            d_ref[low:high, low:high], mm(l_ref[low:high, 0:low], d_ref[0:low, 0:low])
        )
        low = high


def across_rows(a, b):
    return lax.dot_general(
        a, b, (((1,), (1,)), ((), ())), precision=HIGH, preferred_element_type=jnp.float32
    )


def own_kernel(side_ref, own_ref, out_ref, l_ref, d_ref):
    height = own_ref.shape[0]
    even = side_ref[0] == 0
    left, right = own_ref[:, 0:height], own_ref[:, height:]
    l_ref[...] = jnp.where(even, left, right)
    invert_into(l_ref, d_ref)
    out_ref[:, 0:height] = jnp.where(even, d_ref[...], left)
    out_ref[:, height:] = jnp.where(even, 0.0, d_ref[...])


def own_inverse(side, own):
    height = own.shape[0]
    square = pltpu.VMEM((height, height), jnp.float32)
    return pl.pallas_call(
        own_kernel,
        in_specs=[pl.BlockSpec(memory_space=pltpu.SMEM), pl.BlockSpec(memory_space=pltpu.VMEM)],
        out_shape=jax.ShapeDtypeStruct(own.shape, jnp.float32),
        scratch_shapes=[square, square],
    )(side, own)


def join_kernel(side_ref, own_ref, other_ref, cross_ref, mine_ref, yours_ref, x_ref, d_ref):
    height = own_ref.shape[0]
    even = side_ref[0] == 0
    own, other = own_ref[...], other_ref[...]
    upper = jnp.where(even, own[:, 0:height], other[:, 0:height])
    lower = jnp.where(even, other, own)
    d_ref[0:height, 0:height] = upper
    d_ref[0:height, height:] = jnp.zeros((height, height), jnp.float32)
    d_ref[height:, height:] = lower[:, height:]
    d_ref[height:, 0:height] = -mm(lower[:, height:], mm(lower[:, 0:height], upper))
    left, right = d_ref[:, 0:height], d_ref[:, height:]
    mine_ref[...] = jnp.where(even, left, right)
    yours_ref[...] = jnp.where(even, right, left)
    x_ref[...] = across_rows(cross_ref[...], d_ref[...])


def join(side, own, other, cross):
    height = own.shape[0]
    tall = jax.ShapeDtypeStruct((2 * height, height), jnp.float32)
    return pl.pallas_call(
        join_kernel,
        in_specs=[pl.BlockSpec(memory_space=pltpu.SMEM)] + [pl.BlockSpec(memory_space=pltpu.VMEM)] * 3,
        out_shape=[tall, tall, jax.ShapeDtypeStruct(cross.shape, jnp.float32)],
        scratch_shapes=[pltpu.VMEM((2 * height, 2 * height), jnp.float32)],
    )(side, own, other, cross)


def shards(archive_inputs, candidate_inputs, lengthscales, factor):
    height = factor.shape[0]
    width = candidate_inputs.shape[1]
    chain = lax.axis_size("chain")
    cand = lax.axis_size("cand")
    quads = chain // QUAD
    position = lax.axis_index("chain")
    inside = [[QUAD * g + i for i in range(QUAD)] for g in range(quads)]
    across = [[QUAD * g + i for g in range(quads)] for i in range(QUAD)]
    layers = chain // 2
    layer, side = position // 2, position % 2
    odd = layer % 2
    side_word = jnp.full((1,), side, jnp.int32)
    pair_all = [(p, p ^ 1) for p in range(chain)]
    scaling = 1.0 / lengthscales
    scaled_candidates = candidate_inputs * scaling[:, None]

    def both(own, other, axis):
        return jnp.where(
            side == 0,
            jnp.concatenate([own, other], axis=axis),
            jnp.concatenate([other, own], axis=axis),
        )

    def after(value, *events):
        return lax.optimization_barrier((value, *events))[0]

    other_archive = lax.ppermute(archive_inputs, "chain", pair_all)
    own_diagonal = lax.dynamic_slice_in_dim(factor, layer * 2 * height, 2 * height, 1)
    own_part = own_inverse(side_word, own_diagonal)
    other_part = lax.ppermute(own_part, "chain", pair_all)
    half = width // 2
    columns = lax.dynamic_slice_in_dim(scaled_candidates, side * half, half, 1)
    cross = matern(columns, both(archive_inputs, other_archive, 1) * scaling[:, None])
    for_mine, for_yours, solved = join(side_word, own_part, other_part, cross)

    def hop(value, pairs):
        return lax.ppermute(value, "chain", [(2 * a + i, 2 * b + i) for a, b in pairs for i in range(2)])

    span = 2 * height
    core = lax.axis_index("cand") % 2
    chunks = [factor[:, k * span : (k + 1) * span] for k in range(layers)]
    lefts, rights = [], []
    for s in range(layers // 2):
        left = jnp.where(odd == 1, chunks[max(2 * s - 1, 0)], chunks[2 * s])
        right = jnp.where(odd == 1, chunks[2 * s], chunks[2 * s + 1])
        sent = after(jnp.where(core == 0, left, right), other_part if s == 0 else solved)
        got = lax.ppermute(sent, "chain", [(p, p ^ 1) for p in range(chain) if p // 2 >= 2 * s + 1])
        users = [p for p in range(chain) if p // 2 >= 2 * s + 1]
        twins = [(p * cand + c, p * cand + (c ^ 1)) for p in users for c in range(cand)]
        twin = lax.ppermute(got, ("chain", "cand"), twins)
        yours_left = jnp.where(core == 0, got, twin)
        yours_right = jnp.where(core == 0, twin, got)
        mine = jnp.concatenate([left, right], axis=1)
        yours = jnp.concatenate([yours_left, yours_right], axis=1)
        slab = mm(for_mine, mine) + mm(for_yours, yours)
        lefts.append(after(slab[:, :span]))
        rights.append(after(slab[:, span:]))

    far = None
    for t in range(layers - 1):
        near = hop(solved, [(t - k, t + 1 + k) for k in range(layers) if t - k >= 0 and t + 1 + k < layers])
        pairs = [(t - k, t + 2 + k) for k in range(layers) if t - k >= 0 and t + 2 + k < layers]
        ahead = hop(solved, pairs) if pairs else None
        users = sorted({t - z // 2 for z in range(t + 1, min(2 * t + 1, layers - 1) + 1)})
        left, right = lefts[users[0]], rights[users[0]]
        if len(users) > 1:
            second = t - layer // 2 == users[1]
            left = after(jnp.where(second, lefts[users[1]], left))
            right = after(jnp.where(second, rights[users[1]], right))
        if far is not None:
            solved = after(solved - across_rows(far, left))
        solved = solved - across_rows(near, right)
        far = ahead
    other = lax.ppermute(solved, "chain", pair_all)
    rows = jnp.where(
        side == 0,
        jnp.concatenate([solved[:, :height], other[:, :height]], axis=0),
        jnp.concatenate([other[:, height:], solved[:, height:]], axis=0),
    ).T
    swap = [(a * cand + b, b * cand + a) for a in range(chain) for b in range(cand)]
    chosen = lax.ppermute(candidate_inputs, ("chain", "cand"), swap)

    turn = [
        ((QUAD * g + (i ^ j)) * cand + QUAD * m + i, (QUAD * g + i) * cand + QUAD * j + m)
        for g in range(quads)
        for i in range(QUAD)
        for j in range(QUAD)
        for m in range(cand // QUAD)
    ]
    turned = lax.ppermute(rows, ("chain", "cand"), turn)
    mine = [rows]
    for r in range(1, QUAD):
        pairs = [(QUAD * g + i, QUAD * g + (i ^ r)) for g in range(quads) for i in range(QUAD)]
        mine.append(lax.ppermute(rows, "chain", pairs))
    copies = jnp.broadcast_to(turned[None], (cand,) + turned.shape)
    others = lax.all_to_all(copies, "cand", 0, 0, tiled=True)
    others = others.reshape(QUAD, cand // QUAD, height, width)
    shares = jnp.einsum(
        "jmra,jrb->mab", others, jnp.stack(mine), precision=HIGH, preferred_element_type=jnp.float32
    )
    shared = lax.all_to_all(shares, "chain", 0, 0, axis_index_groups=across, tiled=True).sum(axis=0)
    prior_cov = matern(chosen * scaling[:, None], scaled_candidates)
    return (rows, prior_cov - shared)


def solution(mesh):
    return jax.shard_map(
        shards,
        mesh=mesh,
        in_specs=(P(None, "chain"), P(None, "cand"), P(), P("chain", None)),
        out_specs=(P("chain", "cand"), P("chain", "cand")),
        check_vma=False,
    )
```

```python
import jax
import jax.numpy as jnp
from jax import lax
from jax.experimental import pallas as pl
from jax.experimental.pallas import tpu as pltpu
from jax.sharding import PartitionSpec as P

FULL = lax.Precision.HIGHEST
BASE = 32


def matern(first_set, second_set):
    differ = first_set[:, :, None] - second_set[:, None, :]
    radius = jnp.sqrt(5.0 * jnp.sum(differ * differ, axis=0))
    return (1.0 + radius + radius * radius / 3.0) * jnp.exp(-radius)


def mm(a, b):
    return jnp.dot(a, b, precision=FULL, preferred_element_type=jnp.float32)


def quick(a, b, contract=0):
    return lax.dot_general(
        a,
        b,
        (((1,), (contract,)), ((), ())),
        precision=lax.Precision.HIGH,
        preferred_element_type=jnp.float32,
    )


def invert_into(l_ref, d_ref):
    size = l_ref.shape[0]
    count = size // BASE
    rows = lax.broadcasted_iota(jnp.int32, (BASE, BASE), 0)
    cols = lax.broadcasted_iota(jnp.int32, (BASE, BASE), 1)
    strict, solved = [], []
    for k in range(count):
        block = l_ref[k * BASE : (k + 1) * BASE, k * BASE : (k + 1) * BASE]
        diag = jnp.sum(jnp.where(rows == cols, block, 0.0), axis=1, keepdims=True)
        inv = 1.0 / diag
        strict.append(jnp.where(rows > cols, block * inv, 0.0))
        solved.append(jnp.where(rows == cols, inv, 0.0))
    for r in range(BASE - 1):
        for k in range(count):
            solved[k] = solved[k] - strict[k][:, r : r + 1] * solved[k][r : r + 1, :]
    d_ref[...] = jnp.zeros_like(d_ref)
    for k in range(count):
        d_ref[k * BASE : (k + 1) * BASE, k * BASE : (k + 1) * BASE] = solved[k]
    for k in range(0, count - 1, 2):
        a, b, c = k * BASE, (k + 1) * BASE, (k + 2) * BASE
        d_ref[b:c, a:b] = -mm(solved[k + 1], mm(l_ref[b:c, a:b], solved[k]))
    low = 2 * BASE
    while low < size:
        high = low + 2 * BASE
        d_ref[low:high, 0:low] = -mm(
            d_ref[low:high, low:high], mm(l_ref[low:high, 0:low], d_ref[0:low, 0:low])
        )
        low = high


def across_rows(a, b):
    return lax.dot_general(
        a, b, (((1,), (1,)), ((), ())), precision=FULL, preferred_element_type=jnp.float32
    )


def own_kernel(side_ref, own_ref, out_ref, l_ref, d_ref):
    height = own_ref.shape[0]
    even = side_ref[0] == 0
    left, right = own_ref[:, 0:height], own_ref[:, height:]
    l_ref[...] = jnp.where(even, left, right)
    invert_into(l_ref, d_ref)
    out_ref[:, 0:height] = jnp.where(even, d_ref[...], left)
    out_ref[:, height:] = jnp.where(even, 0.0, d_ref[...])


def own_inverse(side, own):
    height = own.shape[0]
    square = pltpu.VMEM((height, height), jnp.float32)
    return pl.pallas_call(
        own_kernel,
        in_specs=[pl.BlockSpec(memory_space=pltpu.SMEM), pl.BlockSpec(memory_space=pltpu.VMEM)],
        out_shape=jax.ShapeDtypeStruct(own.shape, jnp.float32),
        scratch_shapes=[square, square],
    )(side, own)


def join_kernel(side_ref, own_ref, other_ref, cross_ref, mine_ref, yours_ref, x_ref, d_ref):
    height = own_ref.shape[0]
    even = side_ref[0] == 0
    own, other = own_ref[...], other_ref[...]
    upper = jnp.where(even, own[:, 0:height], other[:, 0:height])
    lower = jnp.where(even, other, own)
    d_ref[0:height, 0:height] = upper
    d_ref[0:height, height:] = jnp.zeros((height, height), jnp.float32)
    d_ref[height:, height:] = lower[:, height:]
    d_ref[height:, 0:height] = -mm(lower[:, height:], mm(lower[:, 0:height], upper))
    left, right = d_ref[:, 0:height], d_ref[:, height:]
    mine_ref[...] = jnp.where(even, left, right)
    yours_ref[...] = jnp.where(even, right, left)
    x_ref[...] = across_rows(cross_ref[...], d_ref[...])


def join(side, own, other, cross):
    height = own.shape[0]
    tall = jax.ShapeDtypeStruct((2 * height, height), jnp.float32)
    return pl.pallas_call(
        join_kernel,
        in_specs=[pl.BlockSpec(memory_space=pltpu.SMEM)] + [pl.BlockSpec(memory_space=pltpu.VMEM)] * 3,
        out_shape=[tall, tall, jax.ShapeDtypeStruct(cross.shape, jnp.float32)],
        scratch_shapes=[pltpu.VMEM((2 * height, 2 * height), jnp.float32)],
    )(side, own, other, cross)


def both_of(place, own, other, axis=1):
    return jnp.where(
        place == 0,
        jnp.concatenate([own, other], axis=axis),
        jnp.concatenate([other, own], axis=axis),
    )


def unset(value):
    corner = value[0, 0]
    return (corner != corner).astype(jnp.int32)


def shards(archive_inputs, candidate_inputs, lengthscales, factor):
    height = factor.shape[0]
    width = candidate_inputs.shape[1]
    chain = lax.axis_size("chain")
    cand = lax.axis_size("cand")
    position = lax.axis_index("chain")
    layers = chain // 2
    layer, side = position // 2, position % 2
    odd = layer % 2
    side_word = jnp.full((1,), side, jnp.int32)
    pair_all = [(p, p ^ 1) for p in range(chain)]
    scaling = 1.0 / lengthscales
    scaled_candidates = candidate_inputs * scaling[:, None]

    def both(own, other, axis):
        return both_of(side, own, other, axis)

    def after(value, *events):
        return lax.optimization_barrier((value, *events))[0]

    other_archive = lax.ppermute(archive_inputs, "chain", pair_all)
    own_diagonal = lax.dynamic_slice_in_dim(factor, layer * 2 * height, 2 * height, 1)
    own_part = own_inverse(side_word, own_diagonal)
    other_part = lax.ppermute(own_part, "chain", pair_all)
    half = width // 2
    columns = lax.dynamic_slice_in_dim(scaled_candidates, side * half, half, 1)
    cross = matern(columns, both(archive_inputs, other_archive, 1) * scaling[:, None])
    for_mine, for_yours, solved = join(side_word, own_part, other_part, cross)

    def hop(value, pairs):
        return lax.ppermute(value, "chain", [(2 * a + i, 2 * b + i) for a, b in pairs for i in range(2)])

    span = 2 * height
    core = lax.axis_index("cand") % 2
    late = after(factor, own_part)
    chunks = [late[:, k * span : (k + 1) * span] for k in range(layers)]

    def send(s):
        left = jnp.where(odd == 1, chunks[max(2 * s - 1, 0)], chunks[2 * s])
        right = jnp.where(odd == 1, chunks[2 * s], chunks[2 * s + 1])
        sent = jnp.where(core == 0, left, right)
        sent = after(sent, solved) if s else sent
        got = lax.ppermute(sent, "chain", [(p, p ^ 1) for p in range(chain) if p // 2 >= 2 * s + 1])
        return left, right, got

    def settle(s, left, right, got):
        users = [p for p in range(chain) if p // 2 >= 2 * s + 1]
        twins = [(p * cand + c, p * cand + (c ^ 1)) for p in users for c in range(cand)]
        twin = lax.ppermute(got, ("chain", "cand"), twins)
        yours = jnp.concatenate(
            [jnp.where(core == 0, got, twin), jnp.where(core == 0, twin, got)], axis=1
        )
        slab = quick(for_mine, jnp.concatenate([left, right], axis=1)) + quick(for_yours, yours)
        return after(slab[:, :span]), after(slab[:, span:])

    parts = [send(s) for s in range(layers // 2)]
    slabs = [settle(0, *parts[0][:2], after(parts[0][2], solved))]

    for t in range(layers - 1):
        near = hop(solved, [(t - k, t + 1 + k) for k in range(layers) if t - k >= 0 and t + 1 + k < layers])
        users = sorted({t - z // 2 for z in range(t + 1, min(2 * t + 1, layers - 1) + 1)})
        left, right = slabs[users[0]]
        if len(users) > 1:
            second = t - layer // 2 == users[1]
            left = after(jnp.where(second, slabs[users[1]][0], left))
            right = after(jnp.where(second, slabs[users[1]][1], right))
        if t:
            pairs = [(t - 1 - k, t + 1 + k) for k in range(layers) if t - 1 - k >= 0 and t + 1 + k < layers]
            solved = after(solved - quick(hop(solved, pairs), left, 1))
        solved = solved - quick(near, right, 1)
        if t in (0, 2, 4):
            s = t // 2 + 1
            slabs.append(settle(s, *parts[s][:2], after(parts[s][2], solved)))
        if t == 3:
            wanted = jnp.where(unset(solved) == 0, candidate_inputs, 0.0)
    turn = [
        ((2 * z + h) * cand + 4 * j + 2 * k + y, (2 * z + y) * cand + 4 * j + 2 * h + k)
        for z in range(layers)
        for j in range(cand // 4)
        for h in range(2)
        for k in range(2)
        for y in range(2)
    ]
    turned = lax.ppermute(solved, ("chain", "cand"), turn)
    columns_all = both(solved, lax.ppermute(solved, "chain", pair_all), 0)
    rows = jnp.where(side == 0, columns_all[:, :height], columns_all[:, height:]).T
    twin_columns = lax.ppermute(columns_all, "cand", [(c, c ^ 1) for c in range(cand)])
    same_core = [[2 * i + k for i in range(cand // 2)] for k in range(2)]
    copies = jnp.broadcast_to(turned[None], (cand // 2,) + turned.shape)
    others = lax.all_to_all(copies, "cand", 0, 0, axis_index_groups=same_core, tiled=True)
    swap = [(a * cand + b, b * cand + a) for a in range(chain) for b in range(cand)]
    chosen = lax.ppermute(wanted, ("chain", "cand"), swap)
    prior_cov = matern(chosen * after(scaling, solved)[:, None], scaled_candidates)
    others = others.reshape(cand // 2 * half, span)
    theirs = lax.ppermute(quick(others, twin_columns, 1), "cand", [(c, c ^ 1) for c in range(cand)])
    ours = quick(others, columns_all, 1)
    ours = ours.reshape(layers // 2, 1, width, width)
    theirs = theirs.reshape(layers // 2, 1, width, width)
    shares = both_of(core + unset(prior_cov), ours, theirs).reshape(layers, width, width)
    same_side = [[2 * z + y for z in range(layers)] for y in range(2)]
    shared = lax.all_to_all(shares, "chain", 0, 0, axis_index_groups=same_side, tiled=True).sum(axis=0)
    return (rows, prior_cov - shared)


def solution(mesh):
    return jax.shard_map(
        shards,
        mesh=mesh,
        in_specs=(P(None, "chain"), P(None, "cand"), P(), P("chain", None)),
        out_specs=(P("chain", "cand"), P("chain", "cand")),
        check_vma=False,
    )
```

```python
import jax
import jax.numpy as jnp
from jax import lax
from jax.experimental import pallas as pl
from jax.experimental.pallas import tpu as pltpu
from jax.sharding import PartitionSpec as P


FULL = lax.Precision.HIGHEST
BASE = 32


def matern(first_set, second_set):
    differ = first_set[:, :, None] - second_set[:, None, :]
    radius = jnp.sqrt(5.0 * jnp.sum(differ * differ, axis=0))
    return (1.0 + radius + radius * radius / 3.0) * jnp.exp(-radius)


def mm(a, b):
    return jnp.dot(a, b, precision=FULL, preferred_element_type=jnp.float32)


def quick(a, b, contract=0):
    return lax.dot_general(
        a,
        b,
        (((1,), (contract,)), ((), ())),
        precision=lax.Precision.HIGH,
        preferred_element_type=jnp.float32,
    )


def invert_into(l_ref, d_ref):
    size = l_ref.shape[0]
    count = size // BASE
    rows = lax.broadcasted_iota(jnp.int32, (BASE, BASE), 0)
    cols = lax.broadcasted_iota(jnp.int32, (BASE, BASE), 1)
    strict, solved = [], []
    for k in range(count):
        block = l_ref[k * BASE : (k + 1) * BASE, k * BASE : (k + 1) * BASE]
        diag = jnp.sum(jnp.where(rows == cols, block, 0.0), axis=1, keepdims=True)
        inv = 1.0 / diag
        strict.append(jnp.where(rows > cols, block * inv, 0.0))
        solved.append(jnp.where(rows == cols, inv, 0.0))
    for r in range(BASE - 1):
        for k in range(count):
            solved[k] = solved[k] - strict[k][:, r : r + 1] * solved[k][r : r + 1, :]
    d_ref[...] = jnp.zeros_like(d_ref)
    for k in range(count):
        d_ref[k * BASE : (k + 1) * BASE, k * BASE : (k + 1) * BASE] = solved[k]
    for k in range(0, count - 1, 2):
        a, b, c = k * BASE, (k + 1) * BASE, (k + 2) * BASE
        d_ref[b:c, a:b] = -mm(solved[k + 1], mm(l_ref[b:c, a:b], solved[k]))
    low = 2 * BASE
    while low < size:
        high = low + 2 * BASE
        d_ref[low:high, 0:low] = -mm(
            d_ref[low:high, low:high], mm(l_ref[low:high, 0:low], d_ref[0:low, 0:low])
        )
        low = high


def across_rows(a, b):
    return lax.dot_general(
        a, b, (((1,), (1,)), ((), ())), precision=FULL, preferred_element_type=jnp.float32
    )


def own_kernel(place_ref, own_ref, out_ref, l_ref, d_ref):
    height = own_ref.shape[0]
    even = place_ref[1] == 0
    left, right = own_ref[:, 0:height], own_ref[:, height:]
    l_ref[...] = jnp.where(even, left, right)
    invert_into(l_ref, d_ref)
    out_ref[:, 0:height] = jnp.where(even, d_ref[...], left)
    out_ref[:, height:] = jnp.where(even, 0.0, d_ref[...])


def own_inverse(place, factor):
    height = factor.shape[0]
    square = pltpu.VMEM((height, height), jnp.float32)
    return pl.pallas_call(
        own_kernel,
        grid_spec=pltpu.PrefetchScalarGridSpec(
            num_scalar_prefetch=1,
            grid=(1,),
            in_specs=[pl.BlockSpec((height, 2 * height), lambda _, place: (0, place[0]))],
            out_specs=pl.BlockSpec((height, 2 * height), lambda _, place: (0, 0)),
            scratch_shapes=[square, square],
        ),
        out_shape=jax.ShapeDtypeStruct((height, 2 * height), jnp.float32),
    )(place, factor)


def join_kernel(place_ref, own_ref, other_ref, cross_ref, mine_ref, yours_ref, x_ref, d_ref):
    height = own_ref.shape[0]
    even = place_ref[1] == 0
    own, other = own_ref[...], other_ref[...]
    upper = jnp.where(even, own[:, 0:height], other[:, 0:height])
    lower = jnp.where(even, other, own)
    d_ref[0:height, 0:height] = upper
    d_ref[0:height, height:] = jnp.zeros((height, height), jnp.float32)
    d_ref[height:, height:] = lower[:, height:]
    d_ref[height:, 0:height] = -mm(lower[:, height:], mm(lower[:, 0:height], upper))
    left, right = d_ref[:, 0:height], d_ref[:, height:]
    mine_ref[...] = jnp.where(even, left, right)
    yours_ref[...] = jnp.where(even, right, left)
    x_ref[...] = across_rows(cross_ref[...], d_ref[...])


def join(place, own, other, cross):
    height = own.shape[0]
    tall = jax.ShapeDtypeStruct((2 * height, height), jnp.float32)
    return pl.pallas_call(
        join_kernel,
        in_specs=[pl.BlockSpec(memory_space=pltpu.SMEM)] + [pl.BlockSpec(memory_space=pltpu.VMEM)] * 3,
        out_shape=[tall, tall, jax.ShapeDtypeStruct(cross.shape, jnp.float32)],
        scratch_shapes=[pltpu.VMEM((2 * height, 2 * height), jnp.float32)],
    )(place, own, other, cross)


def both_of(place, own, other, axis=1):
    return jnp.where(
        place == 0,
        jnp.concatenate([own, other], axis=axis),
        jnp.concatenate([other, own], axis=axis),
    )


def unset(value):
    corner = value[0, 0]
    return (corner != corner).astype(jnp.int32)


def shards(archive_inputs, candidate_inputs, lengthscales, factor):
    height = factor.shape[0]
    width = candidate_inputs.shape[1]
    chain = lax.axis_size("chain")
    cand = lax.axis_size("cand")
    position = lax.axis_index("chain")
    layers = chain // 2
    layer, side = position // 2, position % 2
    odd = layer % 2
    place = jnp.stack([layer, side]).astype(jnp.int32)
    pair_all = [(p, p ^ 1) for p in range(chain)]
    scaling = 1.0 / lengthscales
    scaled_candidates = candidate_inputs * scaling[:, None]

    def both(own, other, axis):
        return both_of(side, own, other, axis)

    def after(value, *events):
        return lax.optimization_barrier((value, *events))[0]

    other_archive = lax.ppermute(archive_inputs, "chain", pair_all)
    own_part = own_inverse(place, factor)
    other_part = lax.ppermute(own_part, "chain", pair_all)
    half = width // 2
    columns = lax.dynamic_slice_in_dim(scaled_candidates, side * half, half, 1)
    cross = matern(columns, both(archive_inputs, other_archive, 1) * scaling[:, None])
    for_mine, for_yours, solved = join(place, own_part, other_part, cross)

    def hop(value, pairs):
        return lax.ppermute(value, "chain", [(2 * a + i, 2 * b + i) for a, b in pairs for i in range(2)])

    span = 2 * height
    core = lax.axis_index("cand") % 2
    late = after(factor, own_part)
    chunks = [late[:, k * span : (k + 1) * span] for k in range(layers)]

    def send(s):
        left = jnp.where(odd == 1, chunks[max(2 * s - 1, 0)], chunks[2 * s])
        right = jnp.where(odd == 1, chunks[2 * s], chunks[2 * s + 1])
        sent = jnp.where(core == 0, left, right)
        sent = after(sent, solved) if s else sent
        got = lax.ppermute(sent, "chain", [(p, p ^ 1) for p in range(chain) if p // 2 >= 2 * s + 1])
        return left, right, got

    def settle(s, left, right, got):
        users = [p for p in range(chain) if p // 2 >= 2 * s + 1]
        twins = [(p * cand + c, p * cand + (c ^ 1)) for p in users for c in range(cand)]
        twin = lax.ppermute(got, ("chain", "cand"), twins)
        yours = jnp.concatenate(
            [jnp.where(core == 0, got, twin), jnp.where(core == 0, twin, got)], axis=1
        )
        slab = quick(for_mine, jnp.concatenate([left, right], axis=1)) + quick(for_yours, yours)
        return after(slab[:, :span]), after(slab[:, span:])

    parts = [send(s) for s in range(layers // 2)]
    slabs = [settle(0, *parts[0][:2], after(parts[0][2], solved))]

    far = None
    for t in range(layers - 1):
        near = hop(solved, [(t - k, t + 1 + k) for k in range(layers) if t - k >= 0 and t + 1 + k < layers])
        pairs = [(t - k, t + 2 + k) for k in range(layers) if t - k >= 0 and t + 2 + k < layers]
        if pairs:
            ahead = hop(solved, pairs)
        users = sorted({t - z // 2 for z in range(t + 1, min(2 * t + 1, layers - 1) + 1)})
        left, right = slabs[users[0]]
        if len(users) > 1:
            second = t - layer // 2 == users[1]
            left = after(jnp.where(second, slabs[users[1]][0], left))
            right = after(jnp.where(second, slabs[users[1]][1], right))
        if far is not None:
            solved = after(solved - quick(far, left, 1))
        solved = solved - quick(near, right, 1)
        far = ahead
        if t in (0, 2, 4):
            s = t // 2 + 1
            slabs.append(settle(s, *parts[s][:2], after(parts[s][2], solved)))
        if t == 3:
            wanted = jnp.where(unset(solved) == 0, candidate_inputs, 0.0)
    turn = [
        ((2 * z + h) * cand + 4 * j + 2 * k + y, (2 * z + y) * cand + 4 * j + 2 * h + k)
        for z in range(layers)
        for j in range(cand // 4)
        for h in range(2)
        for k in range(2)
        for y in range(2)
    ]
    turned = lax.ppermute(solved, ("chain", "cand"), turn)
    columns_all = both(solved, lax.ppermute(solved, "chain", pair_all), 0)
    rows = jnp.where(side == 0, columns_all[:, :height], columns_all[:, height:]).T
    twin_columns = lax.ppermute(columns_all, "cand", [(c, c ^ 1) for c in range(cand)])
    same_core = [[2 * i + k for i in range(cand // 2)] for k in range(2)]
    copies = jnp.broadcast_to(turned[None], (cand // 2,) + turned.shape)
    others = lax.all_to_all(copies, "cand", 0, 0, axis_index_groups=same_core, tiled=True)
    swap = [(a * cand + b, b * cand + a) for a in range(chain) for b in range(cand)]
    chosen = lax.ppermute(wanted, ("chain", "cand"), swap)
    prior_cov = matern(chosen * after(scaling, solved)[:, None], scaled_candidates)
    others = others.reshape(cand // 2 * half, span)
    theirs = lax.ppermute(quick(others, twin_columns, 1), "cand", [(c, c ^ 1) for c in range(cand)])
    ours = quick(others, columns_all, 1)
    ours = ours.reshape(layers // 2, 1, width, width)
    theirs = theirs.reshape(layers // 2, 1, width, width)
    shares = both_of(core + unset(prior_cov), ours, theirs).reshape(layers, width, width)
    same_side = [[2 * z + y for z in range(layers)] for y in range(2)]
    shared = lax.all_to_all(shares, "chain", 0, 0, axis_index_groups=same_side, tiled=True).sum(axis=0)
    return (rows, prior_cov - shared)


def solution(mesh):
    return jax.shard_map(
        shards,
        mesh=mesh,
        in_specs=(P(None, "chain"), P(None, "cand"), P(), P("chain", None)),
        out_specs=(P("chain", "cand"), P("chain", "cand")),
        check_vma=False,
    )
```

```python
import jax
import jax.numpy as jnp
from jax import lax
from jax.experimental import pallas as pl
from jax.experimental.pallas import tpu as pltpu
from jax.sharding import PartitionSpec as P


FULL = lax.Precision.HIGHEST
BASE = 32


def matern(first_set, second_set):
    differ = first_set[:, :, None] - second_set[:, None, :]
    radius = jnp.sqrt(5.0 * jnp.sum(differ * differ, axis=0))
    return (1.0 + radius + radius * radius / 3.0) * jnp.exp(-radius)


def mm(a, b):
    return jnp.dot(a, b, precision=FULL, preferred_element_type=jnp.float32)


def quick(a, b, contract=0):
    return lax.dot_general(
        a,
        b,
        (((1,), (contract,)), ((), ())),
        precision=lax.Precision.HIGH,
        preferred_element_type=jnp.float32,
    )


def invert_into(l_ref, d_ref):
    size = l_ref.shape[0]
    count = size // BASE
    rows = lax.broadcasted_iota(jnp.int32, (BASE, BASE), 0)
    cols = lax.broadcasted_iota(jnp.int32, (BASE, BASE), 1)
    strict, solved = [], []
    for k in range(count):
        block = l_ref[k * BASE : (k + 1) * BASE, k * BASE : (k + 1) * BASE]
        diag = jnp.sum(jnp.where(rows == cols, block, 0.0), axis=1, keepdims=True)
        inv = 1.0 / diag
        strict.append(jnp.where(rows > cols, block * inv, 0.0))
        solved.append(jnp.where(rows == cols, inv, 0.0))
    for r in range(BASE - 1):
        for k in range(count):
            solved[k] = solved[k] - strict[k][:, r : r + 1] * solved[k][r : r + 1, :]
    d_ref[...] = jnp.zeros_like(d_ref)
    for k in range(count):
        d_ref[k * BASE : (k + 1) * BASE, k * BASE : (k + 1) * BASE] = solved[k]
    for k in range(0, count - 1, 2):
        a, b, c = k * BASE, (k + 1) * BASE, (k + 2) * BASE
        d_ref[b:c, a:b] = -mm(solved[k + 1], mm(l_ref[b:c, a:b], solved[k]))
    low = 2 * BASE
    while low < size:
        high = low + 2 * BASE
        d_ref[low:high, 0:low] = -mm(
            d_ref[low:high, low:high], mm(l_ref[low:high, 0:low], d_ref[0:low, 0:low])
        )
        low = high


def across_rows(a, b):
    return lax.dot_general(
        a, b, (((1,), (1,)), ((), ())), precision=FULL, preferred_element_type=jnp.float32
    )


def own_kernel(place_ref, own_ref, out_ref, l_ref, d_ref):
    height = own_ref.shape[0]
    even = place_ref[1] == 0
    left, right = own_ref[:, 0:height], own_ref[:, height:]
    l_ref[...] = jnp.where(even, left, right)
    invert_into(l_ref, d_ref)
    out_ref[:, 0:height] = jnp.where(even, d_ref[...], left)
    out_ref[:, height:] = jnp.where(even, 0.0, d_ref[...])


def own_inverse(place, factor):
    height = factor.shape[0]
    square = pltpu.VMEM((height, height), jnp.float32)
    return pl.pallas_call(
        own_kernel,
        grid_spec=pltpu.PrefetchScalarGridSpec(
            num_scalar_prefetch=1,
            grid=(1,),
            in_specs=[pl.BlockSpec((height, 2 * height), lambda _, place: (0, place[0]))],
            out_specs=pl.BlockSpec((height, 2 * height), lambda _, place: (0, 0)),
            scratch_shapes=[square, square],
        ),
        out_shape=jax.ShapeDtypeStruct((height, 2 * height), jnp.float32),
    )(place, factor)


def join_kernel(place_ref, own_ref, other_ref, cross_ref, mine_ref, yours_ref, x_ref, d_ref):
    height = own_ref.shape[0]
    even = place_ref[1] == 0
    own, other = own_ref[...], other_ref[...]
    upper = jnp.where(even, own[:, 0:height], other[:, 0:height])
    lower = jnp.where(even, other, own)
    d_ref[0:height, 0:height] = upper
    d_ref[0:height, height:] = jnp.zeros((height, height), jnp.float32)
    d_ref[height:, height:] = lower[:, height:]
    d_ref[height:, 0:height] = -mm(lower[:, height:], mm(lower[:, 0:height], upper))
    left, right = d_ref[:, 0:height], d_ref[:, height:]
    mine_ref[...] = jnp.where(even, left, right)
    yours_ref[...] = jnp.where(even, right, left)
    x_ref[...] = across_rows(cross_ref[...], d_ref[...])


def join(place, own, other, cross):
    height = own.shape[0]
    tall = jax.ShapeDtypeStruct((2 * height, height), jnp.float32)
    return pl.pallas_call(
        join_kernel,
        in_specs=[pl.BlockSpec(memory_space=pltpu.SMEM)] + [pl.BlockSpec(memory_space=pltpu.VMEM)] * 3,
        out_shape=[tall, tall, jax.ShapeDtypeStruct(cross.shape, jnp.float32)],
        scratch_shapes=[pltpu.VMEM((2 * height, 2 * height), jnp.float32)],
    )(place, own, other, cross)


def both_of(place, own, other, axis=1):
    return jnp.where(
        place == 0,
        jnp.concatenate([own, other], axis=axis),
        jnp.concatenate([other, own], axis=axis),
    )


def unset(value):
    corner = value[0, 0]
    return (corner != corner).astype(jnp.int32)


def shards(archive_inputs, candidate_inputs, lengthscales, factor):
    height = factor.shape[0]
    width = candidate_inputs.shape[1]
    chain = lax.axis_size("chain")
    cand = lax.axis_size("cand")
    position = lax.axis_index("chain")
    layers = chain // 2
    layer, side = position // 2, position % 2
    odd = layer % 2
    place = jnp.stack([layer, side]).astype(jnp.int32)
    pair_all = [(p, p ^ 1) for p in range(chain)]
    scaling = 1.0 / lengthscales
    scaled_candidates = candidate_inputs * scaling[:, None]

    def both(own, other, axis):
        return both_of(side, own, other, axis)

    def after(value, *events):
        return lax.optimization_barrier((value, *events))[0]

    other_archive = lax.ppermute(archive_inputs, "chain", pair_all)
    own_part = own_inverse(place, factor)
    other_part = lax.ppermute(own_part, "chain", pair_all)
    half = width // 2
    columns = lax.dynamic_slice_in_dim(scaled_candidates, side * half, half, 1)
    cross = matern(columns, both(archive_inputs, other_archive, 1) * scaling[:, None])
    for_mine, for_yours, solved = join(place, own_part, other_part, cross)

    def hop(value, pairs):
        return lax.ppermute(value, "chain", [(2 * a + i, 2 * b + i) for a, b in pairs for i in range(2)])

    span = 2 * height
    core = lax.axis_index("cand") % 2
    late = after(factor, own_part)

    def send(s):
        chunks = [(late if s else factor)[:, k * span : (k + 1) * span] for k in range(layers)]
        left = jnp.where(odd == 1, chunks[max(2 * s - 1, 0)], chunks[2 * s])
        right = jnp.where(odd == 1, chunks[2 * s], chunks[2 * s + 1])
        sent = jnp.where(core == 0, left, right)
        sent = after(sent, solved) if s > 1 else sent
        got = lax.ppermute(sent, "chain", [(p, p ^ 1) for p in range(chain) if p // 2 >= 2 * s + 1])
        return left, right, got

    def settle(s, left, right, got):
        users = [p for p in range(chain) if p // 2 >= 2 * s + 1]
        twins = [(p * cand + c, p * cand + (c ^ 1)) for p in users for c in range(cand)]
        twin = lax.ppermute(got, ("chain", "cand"), twins)
        yours = jnp.concatenate(
            [jnp.where(core == 0, got, twin), jnp.where(core == 0, twin, got)], axis=1
        )
        slab = quick(for_mine, jnp.concatenate([left, right], axis=1)) + quick(for_yours, yours)
        return after(slab[:, :span]), after(slab[:, span:])

    parts = [send(s) for s in range(layers // 2)]
    slabs = [settle(0, *parts[0])]

    far = mid = before = None
    for t in range(layers - 1):
        hops = [(k, t - k, t + 1 + k) for k in range(layers) if t - k >= 0 and t + 1 + k < layers]
        near = hop(solved, [(a, b) for k, a, b in hops if k != 1])
        pairs = [(t - k, t + 2 + k) for k in range(layers) if t - k >= 0 and t + 2 + k < layers]
        if pairs:
            ahead = hop(solved, pairs)
        behind = [(a, b) for k, a, b in hops if k == 1]
        if behind:
            behind = hop(solved, behind)
        users = sorted({t - z // 2 for z in range(t + 1, min(2 * t + 1, layers - 1) + 1)})
        left, right = slabs[users[0]]
        if len(users) > 1:
            second = t - layer // 2 == users[1]
            left = after(jnp.where(second, slabs[users[1]][0], left))
            right = after(jnp.where(second, slabs[users[1]][1], right))
        if mid is not None:
            solved = solved - quick(mid, before, 1)
        if far is not None:
            solved = after(solved - quick(far, left, 1))
        solved = solved - quick(near, right, 1)
        far, mid, before = ahead, (behind if len(behind) else None), right
        if t in (0, 2, 4):
            s = t // 2 + 1
            slabs.append(settle(s, *parts[s][:2], after(parts[s][2], solved)))
        if t == 3:
            wanted = jnp.where(unset(solved) == 0, candidate_inputs, 0.0)
    turns = [
        [
            ((2 * z + h) * cand + 8 * k + 2 * x + y, (2 * z + y) * cand + 8 * (h ^ other) + 2 * x + k)
            for z in range(layers)
            for h in range(2)
            for k in range(2)
            for x in range(cand // 4)
            for y in range(2)
        ]
        for other in range(2)
    ]
    turned = [lax.ppermute(solved, ("chain", "cand"), turn) for turn in turns]
    turned = both_of(lax.axis_index("cand") // 8, *turned, 0)
    columns_all = both(solved, lax.ppermute(solved, "chain", pair_all), 0)
    rows = jnp.where(side == 0, columns_all[:, :height], columns_all[:, height:]).T
    twin_columns = lax.ppermute(columns_all, "cand", [(c, c ^ 1) for c in range(cand)])
    same_row = [[8 * j + 2 * x + k for x in range(cand // 4)] for j in range(2) for k in range(2)]
    copies = jnp.broadcast_to(turned[None], (cand // 4,) + turned.shape)
    others = lax.all_to_all(copies, "cand", 0, 0, axis_index_groups=same_row, tiled=True)
    swap = [(a * cand + b, b * cand + a) for a in range(chain) for b in range(cand)]
    chosen = lax.ppermute(wanted, ("chain", "cand"), swap)
    prior_cov = matern(chosen * after(scaling, solved)[:, None], scaled_candidates)
    others = others.reshape(cand // 4 * width, span)
    theirs = lax.ppermute(quick(others, twin_columns, 1), "cand", [(c, c ^ 1) for c in range(cand)])
    ours = quick(others, columns_all, 1)
    shares = both_of(core + unset(prior_cov), ours, theirs, 0).reshape(layers, width, width)
    same_side = [[2 * z + y for z in range(layers)] for y in range(2)]
    shared = lax.all_to_all(shares, "chain", 0, 0, axis_index_groups=same_side, tiled=True).sum(axis=0)
    return (rows, prior_cov - shared)


def solution(mesh):
    return jax.shard_map(
        shards,
        mesh=mesh,
        in_specs=(P(None, "chain"), P(None, "cand"), P(), P("chain", None)),
        out_specs=(P("chain", "cand"), P("chain", "cand")),
        check_vma=False,
    )
```

```python
import jax
import jax.numpy as jnp
from jax import lax
from jax.experimental import pallas as pl
from jax.experimental.pallas import tpu as pltpu
from jax.sharding import PartitionSpec as P


FULL = lax.Precision.HIGHEST
BASE = 32


def matern(first_set, second_set):
    differ = first_set[:, :, None] - second_set[:, None, :]
    radius = jnp.sqrt(5.0 * jnp.sum(differ * differ, axis=0))
    return (1.0 + radius + radius * radius / 3.0) * jnp.exp(-radius)


def mm(a, b):
    return jnp.dot(a, b, precision=FULL, preferred_element_type=jnp.float32)


def quick(a, b, contract=0):
    return lax.dot_general(
        a,
        b,
        (((1,), (contract,)), ((), ())),
        precision=lax.Precision.HIGH,
        preferred_element_type=jnp.float32,
    )


def invert_into(l_ref, d_ref):
    size = l_ref.shape[0]
    count = size // BASE
    rows = lax.broadcasted_iota(jnp.int32, (BASE, BASE), 0)
    cols = lax.broadcasted_iota(jnp.int32, (BASE, BASE), 1)
    strict, solved = [], []
    for k in range(count):
        block = l_ref[k * BASE : (k + 1) * BASE, k * BASE : (k + 1) * BASE]
        diag = jnp.sum(jnp.where(rows == cols, block, 0.0), axis=1, keepdims=True)
        inv = 1.0 / diag
        strict.append(jnp.where(rows > cols, block * inv, 0.0))
        solved.append(jnp.where(rows == cols, inv, 0.0))
    for r in range(BASE - 1):
        for k in range(count):
            solved[k] = solved[k] - strict[k][:, r : r + 1] * solved[k][r : r + 1, :]
    d_ref[...] = jnp.zeros_like(d_ref)
    for k in range(count):
        d_ref[k * BASE : (k + 1) * BASE, k * BASE : (k + 1) * BASE] = solved[k]
    for k in range(0, count - 1, 2):
        a, b, c = k * BASE, (k + 1) * BASE, (k + 2) * BASE
        d_ref[b:c, a:b] = -mm(solved[k + 1], mm(l_ref[b:c, a:b], solved[k]))
    low = 2 * BASE
    while low < size:
        high = low + 2 * BASE
        d_ref[low:high, 0:low] = -mm(
            d_ref[low:high, low:high], mm(l_ref[low:high, 0:low], d_ref[0:low, 0:low])
        )
        low = high


def across_rows(a, b):
    return lax.dot_general(
        a, b, (((1,), (1,)), ((), ())), precision=FULL, preferred_element_type=jnp.float32
    )


def own_kernel(place_ref, own_ref, out_ref, l_ref, d_ref):
    height = own_ref.shape[0]
    even = place_ref[0] % 2 == 0
    left, right = own_ref[:, 0:height], own_ref[:, height:]
    l_ref[...] = jnp.where(even, left, right)
    invert_into(l_ref, d_ref)
    out_ref[:, 0:height] = jnp.where(even, d_ref[...], left)
    out_ref[:, height:] = jnp.where(even, 0.0, d_ref[...])


def own_inverse(place, factor):
    height = factor.shape[0]
    square = pltpu.VMEM((height, height), jnp.float32)
    return pl.pallas_call(
        own_kernel,
        grid_spec=pltpu.PrefetchScalarGridSpec(
            num_scalar_prefetch=1,
            grid=(1,),
            in_specs=[pl.BlockSpec((height, 2 * height), lambda _, place: (0, place[0] // 2))],
            out_specs=pl.BlockSpec((height, 2 * height), lambda _, place: (0, 0)),
            scratch_shapes=[square, square],
        ),
        out_shape=jax.ShapeDtypeStruct((height, 2 * height), jnp.float32),
    )(place, factor)


def join_kernel(place_ref, own_ref, other_ref, cross_ref, mine_ref, yours_ref, x_ref, d_ref):
    height = own_ref.shape[0]
    even = place_ref[0] % 2 == 0
    own, other = own_ref[...], other_ref[...]
    upper = jnp.where(even, own[:, 0:height], other[:, 0:height])
    lower = jnp.where(even, other, own)
    d_ref[0:height, 0:height] = upper
    d_ref[0:height, height:] = jnp.zeros((height, height), jnp.float32)
    d_ref[height:, height:] = lower[:, height:]
    d_ref[height:, 0:height] = -mm(lower[:, height:], mm(lower[:, 0:height], upper))
    left, right = d_ref[:, 0:height], d_ref[:, height:]
    mine_ref[...] = jnp.where(even, left, right)
    yours_ref[...] = jnp.where(even, right, left)
    x_ref[...] = across_rows(cross_ref[...], d_ref[...])


def join(place, own, other, cross):
    height = own.shape[0]
    tall = jax.ShapeDtypeStruct((2 * height, height), jnp.float32)
    return pl.pallas_call(
        join_kernel,
        in_specs=[pl.BlockSpec(memory_space=pltpu.SMEM)] + [pl.BlockSpec(memory_space=pltpu.VMEM)] * 3,
        out_shape=[tall, tall, jax.ShapeDtypeStruct(cross.shape, jnp.float32)],
        scratch_shapes=[pltpu.VMEM((2 * height, 2 * height), jnp.float32)],
    )(place, own, other, cross)


def both_of(place, own, other, axis=1):
    return jnp.where(
        place == 0,
        jnp.concatenate([own, other], axis=axis),
        jnp.concatenate([other, own], axis=axis),
    )


def unset(value):
    corner = value[0, 0]
    return (corner != corner).astype(jnp.int32)


def shards(archive_inputs, candidate_inputs, lengthscales, factor):
    height = factor.shape[0]
    width = candidate_inputs.shape[1]
    chain = lax.axis_size("chain")
    cand = lax.axis_size("cand")
    position = lax.axis_index("chain")
    layers = chain // 2
    layer, side = position // 2, position % 2
    odd = layer % 2
    place = jnp.full((1,), position, jnp.int32)
    pair_all = [(p, p ^ 1) for p in range(chain)]
    scaling = 1.0 / lengthscales
    scaled_candidates = candidate_inputs * scaling[:, None]

    def both(own, other, axis):
        return both_of(side, own, other, axis)

    def after(value, *events):
        return lax.optimization_barrier((value, *events))[0]

    other_archive = lax.ppermute(archive_inputs, "chain", pair_all)
    own_part = own_inverse(place, factor)
    other_part = lax.ppermute(own_part, "chain", pair_all)
    half = width // 2
    columns = lax.dynamic_slice_in_dim(scaled_candidates, side * half, half, 1)
    cross = matern(columns, both(archive_inputs, other_archive, 1) * scaling[:, None])
    for_mine, for_yours, solved = join(place, own_part, other_part, cross)

    def hop(value, pairs):
        return lax.ppermute(value, "chain", [(2 * a + i, 2 * b + i) for a, b in pairs for i in range(2)])

    span = 2 * height
    core = lax.axis_index("cand") % 2
    late = after(factor, own_part)

    def send(s):
        chunks = [(late if s else factor)[:, k * span : (k + 1) * span] for k in range(layers)]
        left = jnp.where(odd == 1, chunks[max(2 * s - 1, 0)], chunks[2 * s])
        right = jnp.where(odd == 1, chunks[2 * s], chunks[2 * s + 1])
        sent = jnp.where(core == 0, left, right)
        sent = after(sent, solved) if s else sent
        got = lax.ppermute(sent, "chain", [(p, p ^ 1) for p in range(chain) if p // 2 >= 2 * s + 1])
        return left, right, got

    def share(s, got):
        users = [p for p in range(chain) if p // 2 >= 2 * s + 1]
        twins = [(p * cand + c, p * cand + (c ^ 1)) for p in users for c in range(cand)]
        twin = lax.ppermute(got, ("chain", "cand"), twins)
        return jnp.where(core == 0, got, twin), jnp.where(core == 0, twin, got)

    def settle(left, right, yours_left, yours_right):
        yours = jnp.concatenate([yours_left, yours_right], axis=1)
        slab = quick(for_mine, jnp.concatenate([left, right], axis=1)) + quick(for_yours, yours)
        return after(slab[:, :span]), after(slab[:, span:])

    parts = [send(s) for s in range(layers // 2)]
    slabs = [settle(*parts[s][:2], *share(s, parts[s][2])) for s in range(2)]
    shared_parts = {}

    far = mid = before = None
    for t in range(layers - 1):
        hops = [(k, t - k, t + 1 + k) for k in range(layers) if t - k >= 0 and t + 1 + k < layers]
        near = hop(solved, [(a, b) for k, a, b in hops if k != 1])
        pairs = [(t - k, t + 2 + k) for k in range(layers) if t - k >= 0 and t + 2 + k < layers]
        if pairs:
            ahead = hop(solved, pairs)
        behind = [(a, b) for k, a, b in hops if k == 1]
        if behind:
            behind = hop(solved, behind)
        users = sorted({t - z // 2 for z in range(t + 1, min(2 * t + 1, layers - 1) + 1)})
        left, right = slabs[users[0]]
        if len(users) > 1:
            second = t - layer // 2 == users[1]
            left = after(jnp.where(second, slabs[users[1]][0], left))
            right = after(jnp.where(second, slabs[users[1]][1], right))
        if mid is not None:
            solved = solved - quick(mid, before, 1)
        if far is not None:
            solved = after(solved - quick(far, left, 1))
        solved = solved - quick(near, right, 1)
        far, mid, before = ahead, (behind if len(behind) else None), right
        if t in (1, 2):
            shared_parts[t + 1] = share(t + 1, after(parts[t + 1][2], solved))
        if t in (2, 3):
            slabs.append(settle(*parts[t][:2], *(after(part, solved) for part in shared_parts[t])))
        if t == 3:
            wanted = jnp.where(unset(solved) == 0, candidate_inputs, 0.0)
    turns = [
        [
            ((2 * z + h) * cand + 8 * k + 2 * x + y, (2 * z + y) * cand + 8 * (h ^ other) + 2 * x + k)
            for z in range(layers)
            for h in range(2)
            for k in range(2)
            for x in range(cand // 4)
            for y in range(2)
        ]
        for other in range(2)
    ]
    turned = [lax.ppermute(solved, ("chain", "cand"), turn) for turn in turns]
    turned = both_of(lax.axis_index("cand") // 8, *turned, 0)
    columns_all = both(solved, lax.ppermute(solved, "chain", pair_all), 0)
    rows = jnp.where(side == 0, columns_all[:, :height], columns_all[:, height:]).T
    twin_columns = lax.ppermute(columns_all, "cand", [(c, c ^ 1) for c in range(cand)])
    same_row = [[8 * j + 2 * x + k for x in range(cand // 4)] for j in range(2) for k in range(2)]
    copies = jnp.broadcast_to(turned[None], (cand // 4,) + turned.shape)
    others = lax.all_to_all(copies, "cand", 0, 0, axis_index_groups=same_row, tiled=True)
    swap = [(a * cand + b, b * cand + a) for a in range(chain) for b in range(cand)]
    chosen = lax.ppermute(wanted, ("chain", "cand"), swap)
    prior_cov = matern(chosen * after(scaling, solved)[:, None], scaled_candidates)
    others = others.reshape(cand // 4 * width, span)
    theirs = lax.ppermute(quick(others, twin_columns, 1), "cand", [(c, c ^ 1) for c in range(cand)])
    ours = quick(others, columns_all, 1)
    shares = both_of(core + unset(prior_cov), ours, theirs, 0).reshape(layers, width, width)
    same_side = [[2 * z + y for z in range(layers)] for y in range(2)]
    shared = lax.all_to_all(shares, "chain", 0, 0, axis_index_groups=same_side, tiled=True).sum(axis=0)
    return (rows, prior_cov - shared)


def solution(mesh):
    return jax.shard_map(
        shards,
        mesh=mesh,
        in_specs=(P(None, "chain"), P(None, "cand"), P(), P("chain", None)),
        out_specs=(P("chain", "cand"), P("chain", "cand")),
        check_vma=False,
    )
```

```python
import jax
import jax.numpy as jnp
from jax import lax
from jax.experimental import pallas as pl
from jax.experimental.pallas import tpu as pltpu
from jax.sharding import PartitionSpec as P


FULL = lax.Precision.HIGHEST
BASE = 32


def matern(first_set, second_set):
    differ = first_set[:, :, None] - second_set[:, None, :]
    radius = jnp.sqrt(5.0 * jnp.sum(differ * differ, axis=0))
    return (1.0 + radius + radius * radius / 3.0) * jnp.exp(-radius)


def mm(a, b):
    return jnp.dot(a, b, precision=FULL, preferred_element_type=jnp.float32)


def quick(a, b, contract=0):
    return lax.dot_general(
        a,
        b,
        (((1,), (contract,)), ((), ())),
        precision=lax.Precision.HIGH,
        preferred_element_type=jnp.float32,
    )


def invert_into(l_ref, d_ref):
    size = l_ref.shape[0]
    count = size // BASE
    rows = lax.broadcasted_iota(jnp.int32, (BASE, BASE), 0)
    cols = lax.broadcasted_iota(jnp.int32, (BASE, BASE), 1)
    strict, solved = [], []
    for k in range(count):
        block = l_ref[k * BASE : (k + 1) * BASE, k * BASE : (k + 1) * BASE]
        diag = jnp.sum(jnp.where(rows == cols, block, 0.0), axis=1, keepdims=True)
        inv = 1.0 / diag
        strict.append(jnp.where(rows > cols, block * inv, 0.0))
        solved.append(jnp.where(rows == cols, inv, 0.0))
    for r in range(BASE - 1):
        for k in range(count):
            solved[k] = solved[k] - strict[k][:, r : r + 1] * solved[k][r : r + 1, :]
    d_ref[...] = jnp.zeros_like(d_ref)
    for k in range(count):
        d_ref[k * BASE : (k + 1) * BASE, k * BASE : (k + 1) * BASE] = solved[k]
    for k in range(0, count - 1, 2):
        a, b, c = k * BASE, (k + 1) * BASE, (k + 2) * BASE
        d_ref[b:c, a:b] = -mm(solved[k + 1], mm(l_ref[b:c, a:b], solved[k]))
    low = 2 * BASE
    while low < size:
        high = low + 2 * BASE
        d_ref[low:high, 0:low] = -mm(
            d_ref[low:high, low:high], mm(l_ref[low:high, 0:low], d_ref[0:low, 0:low])
        )
        low = high


def across_rows(a, b):
    return lax.dot_general(
        a, b, (((1,), (1,)), ((), ())), precision=FULL, preferred_element_type=jnp.float32
    )


def own_kernel(place_ref, own_ref, out_ref, l_ref, d_ref):
    height = own_ref.shape[0]
    even = place_ref[0] % 2 == 0
    left, right = own_ref[:, 0:height], own_ref[:, height:]
    l_ref[...] = jnp.where(even, left, right)
    invert_into(l_ref, d_ref)
    out_ref[:, 0:height] = jnp.where(even, d_ref[...], left)
    out_ref[:, height:] = jnp.where(even, 0.0, d_ref[...])


def own_inverse(place, factor):
    height = factor.shape[0]
    square = pltpu.VMEM((height, height), jnp.float32)
    return pl.pallas_call(
        own_kernel,
        grid_spec=pltpu.PrefetchScalarGridSpec(
            num_scalar_prefetch=1,
            grid=(1,),
            in_specs=[pl.BlockSpec((height, 2 * height), lambda _, place: (0, place[0] // 2))],
            out_specs=pl.BlockSpec((height, 2 * height), lambda _, place: (0, 0)),
            scratch_shapes=[square, square],
        ),
        out_shape=jax.ShapeDtypeStruct((height, 2 * height), jnp.float32),
    )(place, factor)


def join_kernel(place_ref, own_ref, other_ref, cross_ref, mine_ref, yours_ref, x_ref, d_ref):
    height = own_ref.shape[0]
    even = place_ref[0] % 2 == 0
    own, other = own_ref[...], other_ref[...]
    upper = jnp.where(even, own[:, 0:height], other[:, 0:height])
    lower = jnp.where(even, other, own)
    d_ref[0:height, 0:height] = upper
    d_ref[0:height, height:] = jnp.zeros((height, height), jnp.float32)
    d_ref[height:, height:] = lower[:, height:]
    d_ref[height:, 0:height] = -mm(lower[:, height:], mm(lower[:, 0:height], upper))
    left, right = d_ref[:, 0:height], d_ref[:, height:]
    mine_ref[...] = jnp.where(even, left, right)
    yours_ref[...] = jnp.where(even, right, left)
    x_ref[...] = across_rows(cross_ref[...], d_ref[...])


def join(place, own, other, cross):
    height = own.shape[0]
    tall = jax.ShapeDtypeStruct((2 * height, height), jnp.float32)
    return pl.pallas_call(
        join_kernel,
        in_specs=[pl.BlockSpec(memory_space=pltpu.SMEM)] + [pl.BlockSpec(memory_space=pltpu.VMEM)] * 3,
        out_shape=[tall, tall, jax.ShapeDtypeStruct(cross.shape, jnp.float32)],
        scratch_shapes=[pltpu.VMEM((2 * height, 2 * height), jnp.float32)],
    )(place, own, other, cross)


def both_of(place, own, other, axis=1):
    return jnp.where(
        place == 0,
        jnp.concatenate([own, other], axis=axis),
        jnp.concatenate([other, own], axis=axis),
    )


def unset(value):
    corner = value[0, 0]
    return (corner != corner).astype(jnp.int32)


def shards(archive_inputs, candidate_inputs, lengthscales, factor):
    height = factor.shape[0]
    width = candidate_inputs.shape[1]
    chain = lax.axis_size("chain")
    cand = lax.axis_size("cand")
    position = lax.axis_index("chain")
    layers = chain // 2
    layer, side = position // 2, position % 2
    odd = layer % 2
    place = jnp.full((1,), position, jnp.int32)
    pair_all = [(p, p ^ 1) for p in range(chain)]
    scaling = 1.0 / lengthscales
    scaled_candidates = candidate_inputs * scaling[:, None]

    def both(own, other, axis):
        return both_of(side, own, other, axis)

    def after(value, *events):
        return lax.optimization_barrier((value, *events))[0]

    other_archive = lax.ppermute(archive_inputs, "chain", pair_all)
    own_part = own_inverse(place, factor)
    other_part = lax.ppermute(own_part, "chain", pair_all)
    half = width // 2
    columns = lax.dynamic_slice_in_dim(scaled_candidates, side * half, half, 1)
    cross = matern(columns, both(archive_inputs, other_archive, 1) * scaling[:, None])
    for_mine, for_yours, solved = join(place, own_part, other_part, cross)

    def hop(value, pairs):
        return lax.ppermute(value, "chain", [(2 * a + i, 2 * b + i) for a, b in pairs for i in range(2)])

    span = 2 * height
    core = lax.axis_index("cand") % 2
    late = after(factor, own_part)

    def send(s):
        chunks = [(late if s else factor)[:, k * span : (k + 1) * span] for k in range(layers)]
        left = jnp.where(odd == 1, chunks[max(2 * s - 1, 0)], chunks[2 * s])
        right = jnp.where(odd == 1, chunks[2 * s], chunks[2 * s + 1])
        mine = jnp.concatenate([left, right], axis=1)
        sent = after(mine, solved) if s else jnp.where(core == 0, left, right)
        got = lax.ppermute(sent, "chain", [(p, p ^ 1) for p in range(chain) if p // 2 >= 2 * s + 1])
        return mine, got

    def share(s, got):
        users = [p for p in range(chain) if p // 2 >= 2 * s + 1]
        twins = [(p * cand + c, p * cand + (c ^ 1)) for p in users for c in range(cand)]
        twin = lax.ppermute(got, ("chain", "cand"), twins)
        return jnp.concatenate(
            [jnp.where(core == 0, got, twin), jnp.where(core == 0, twin, got)], axis=1
        )

    def settle(mine, yours):
        slab = quick(for_mine, mine) + quick(for_yours, yours)
        return after(slab[:, :span]), after(slab[:, span:])

    parts = [send(s) for s in range(layers // 2)]
    slabs = [settle(parts[0][0], share(0, parts[0][1])), settle(*parts[1])]

    far = mid = before = None
    for t in range(layers - 1):
        hops = [(k, t - k, t + 1 + k) for k in range(layers) if t - k >= 0 and t + 1 + k < layers]
        near = hop(solved, [(a, b) for k, a, b in hops if k != 1])
        pairs = [(t - k, t + 2 + k) for k in range(layers) if t - k >= 0 and t + 2 + k < layers]
        if pairs:
            ahead = hop(solved, pairs)
        behind = [(a, b) for k, a, b in hops if k == 1]
        if behind:
            behind = hop(solved, behind)
        users = sorted({t - z // 2 for z in range(t + 1, min(2 * t + 1, layers - 1) + 1)})
        left, right = slabs[users[0]]
        if len(users) > 1:
            second = t - layer // 2 == users[1]
            left = after(jnp.where(second, slabs[users[1]][0], left))
            right = after(jnp.where(second, slabs[users[1]][1], right))
        if mid is not None:
            solved = solved - quick(mid, before, 1)
        if far is not None:
            solved = after(solved - quick(far, left, 1))
        solved = solved - quick(near, right, 1)
        far, mid, before = ahead, (behind if len(behind) else None), right
        if t in (2, 3):
            slabs.append(settle(parts[t][0], after(parts[t][1], solved)))
        if t == 3:
            wanted = jnp.where(unset(solved) == 0, candidate_inputs, 0.0)
    turns = [
        [
            ((2 * z + h) * cand + 8 * k + 2 * x + y, (2 * z + y) * cand + 8 * (h ^ other) + 2 * x + k)
            for z in range(layers)
            for h in range(2)
            for k in range(2)
            for x in range(cand // 4)
            for y in range(2)
        ]
        for other in range(2)
    ]
    turned = []
    for turn in turns:
        turned.append(lax.ppermute(solved, ("chain", "cand"), turn))
    turned = both_of(lax.axis_index("cand") // 8, *turned, 0)
    other_columns = lax.ppermute(solved, "chain", pair_all)
    columns_all = both(solved, other_columns, 0)
    rows = jnp.where(side == 0, columns_all[:, :height], columns_all[:, height:]).T
    twin_columns = lax.ppermute(columns_all, "cand", [(c, c ^ 1) for c in range(cand)])
    row = lax.axis_index("cand") // 2 % (cand // 4)
    others = [turned]
    for r in range(1, cand // 4):
        others.append(lax.ppermute(turned, "cand", [(c, c ^ (2 * r)) for c in range(cand)]))
    others = both_of(row // 2, jnp.stack(others[:2]), jnp.stack(others[2:]), 0).reshape(2, 2, width, span)
    others = both_of(row % 2, others[:, :1], others[:, 1:])
    swap = [(a * cand + b, b * cand + a) for a in range(chain) for b in range(cand)]
    chosen = lax.ppermute(wanted, ("chain", "cand"), swap)
    prior_cov = matern(chosen * after(scaling, solved)[:, None], scaled_candidates)
    others = others.reshape(cand // 4 * width, span)
    theirs = lax.ppermute(quick(others, twin_columns, 1), "cand", [(c, c ^ 1) for c in range(cand)])
    ours = quick(others, columns_all, 1)
    shares = both_of(core + unset(prior_cov), ours, theirs, 0).reshape(layers, width, width)
    same_side = [[2 * z + y for z in range(layers)] for y in range(2)]
    shared = lax.all_to_all(shares, "chain", 0, 0, axis_index_groups=same_side, tiled=True).sum(axis=0)
    return (rows, prior_cov - shared)


def solution(mesh):
    return jax.shard_map(
        shards,
        mesh=mesh,
        in_specs=(P(None, "chain"), P(None, "cand"), P(), P("chain", None)),
        out_specs=(P("chain", "cand"), P("chain", "cand")),
        check_vma=False,
    )
```

```python
import jax
import jax.numpy as jnp
from jax import lax
from jax.experimental import pallas as pl
from jax.experimental.pallas import tpu as pltpu
from jax.sharding import PartitionSpec as P


FULL = lax.Precision.HIGHEST
BASE = 32


def matern(first_set, second_set):
    differ = first_set[:, :, None] - second_set[:, None, :]
    radius = jnp.sqrt(5.0 * jnp.sum(differ * differ, axis=0))
    return (1.0 + radius + radius * radius / 3.0) * jnp.exp(-radius)


def mm(a, b):
    return jnp.dot(a, b, precision=FULL, preferred_element_type=jnp.float32)


def quick(a, b, contract=0):
    return lax.dot_general(
        a,
        b,
        (((1,), (contract,)), ((), ())),
        precision=lax.Precision.HIGH,
        preferred_element_type=jnp.float32,
    )


def invert_into(l_ref, d_ref):
    size = l_ref.shape[0]
    count = size // BASE
    rows = lax.broadcasted_iota(jnp.int32, (BASE, BASE), 0)
    cols = lax.broadcasted_iota(jnp.int32, (BASE, BASE), 1)
    strict, solved = [], []
    for k in range(count):
        block = l_ref[k * BASE : (k + 1) * BASE, k * BASE : (k + 1) * BASE]
        diag = jnp.sum(jnp.where(rows == cols, block, 0.0), axis=1, keepdims=True)
        inv = 1.0 / diag
        strict.append(jnp.where(rows > cols, block * inv, 0.0))
        solved.append(jnp.where(rows == cols, inv, 0.0))
    for r in range(BASE - 1):
        for k in range(count):
            solved[k] = solved[k] - strict[k][:, r : r + 1] * solved[k][r : r + 1, :]
    d_ref[...] = jnp.zeros_like(d_ref)
    for k in range(count):
        d_ref[k * BASE : (k + 1) * BASE, k * BASE : (k + 1) * BASE] = solved[k]
    for k in range(0, count - 1, 2):
        a, b, c = k * BASE, (k + 1) * BASE, (k + 2) * BASE
        d_ref[b:c, a:b] = -mm(solved[k + 1], mm(l_ref[b:c, a:b], solved[k]))
    low = 2 * BASE
    while low < size:
        high = low + 2 * BASE
        d_ref[low:high, 0:low] = -mm(
            d_ref[low:high, low:high], mm(l_ref[low:high, 0:low], d_ref[0:low, 0:low])
        )
        low = high


def across_rows(a, b):
    return lax.dot_general(
        a, b, (((1,), (1,)), ((), ())), precision=FULL, preferred_element_type=jnp.float32
    )


def own_kernel(place_ref, own_ref, out_ref, l_ref, d_ref):
    height = own_ref.shape[0]
    even = place_ref[0] % 2 == 0
    left, right = own_ref[:, 0:height], own_ref[:, height:]
    l_ref[...] = jnp.where(even, left, right)
    invert_into(l_ref, d_ref)
    out_ref[:, 0:height] = jnp.where(even, d_ref[...], left)
    out_ref[:, height:] = jnp.where(even, 0.0, d_ref[...])


def own_inverse(place, factor):
    height = factor.shape[0]
    square = pltpu.VMEM((height, height), jnp.float32)
    return pl.pallas_call(
        own_kernel,
        grid_spec=pltpu.PrefetchScalarGridSpec(
            num_scalar_prefetch=1,
            grid=(1,),
            in_specs=[pl.BlockSpec((height, 2 * height), lambda _, place: (0, place[0] // 2))],
            out_specs=pl.BlockSpec((height, 2 * height), lambda _, place: (0, 0)),
            scratch_shapes=[square, square],
        ),
        out_shape=jax.ShapeDtypeStruct((height, 2 * height), jnp.float32),
    )(place, factor)


def join_kernel(place_ref, own_ref, other_ref, cross_ref, mine_ref, yours_ref, x_ref, d_ref):
    height = own_ref.shape[0]
    even = place_ref[0] % 2 == 0
    own, other = own_ref[...], other_ref[...]
    upper = jnp.where(even, own[:, 0:height], other[:, 0:height])
    lower = jnp.where(even, other, own)
    d_ref[0:height, 0:height] = upper
    d_ref[0:height, height:] = jnp.zeros((height, height), jnp.float32)
    d_ref[height:, height:] = lower[:, height:]
    d_ref[height:, 0:height] = -mm(lower[:, height:], mm(lower[:, 0:height], upper))
    left, right = d_ref[:, 0:height], d_ref[:, height:]
    mine_ref[...] = jnp.where(even, left, right)
    yours_ref[...] = jnp.where(even, right, left)
    x_ref[...] = across_rows(cross_ref[...], d_ref[...])


def join(place, own, other, cross):
    height = own.shape[0]
    tall = jax.ShapeDtypeStruct((2 * height, height), jnp.float32)
    return pl.pallas_call(
        join_kernel,
        in_specs=[pl.BlockSpec(memory_space=pltpu.SMEM)] + [pl.BlockSpec(memory_space=pltpu.VMEM)] * 3,
        out_shape=[tall, tall, jax.ShapeDtypeStruct(cross.shape, jnp.float32)],
        scratch_shapes=[pltpu.VMEM((2 * height, 2 * height), jnp.float32)],
    )(place, own, other, cross)


def both_of(place, own, other, axis=1):
    return jnp.where(
        place == 0,
        jnp.concatenate([own, other], axis=axis),
        jnp.concatenate([other, own], axis=axis),
    )


def unset(value):
    corner = value[0, 0]
    return (corner != corner).astype(jnp.int32)


def shards(archive_inputs, candidate_inputs, lengthscales, factor):
    height = factor.shape[0]
    width = candidate_inputs.shape[1]
    chain = lax.axis_size("chain")
    cand = lax.axis_size("cand")
    position = lax.axis_index("chain")
    layers = chain // 2
    layer, side = position // 2, position % 2
    odd = layer % 2
    place = jnp.full((1,), position, jnp.int32)
    pair_all = [(p, p ^ 1) for p in range(chain)]
    scaling = 1.0 / lengthscales
    scaled_candidates = candidate_inputs * scaling[:, None]

    def both(own, other, axis):
        return both_of(side, own, other, axis)

    def after(value, *events):
        return lax.optimization_barrier((value, *events))[0]

    other_archive = lax.ppermute(archive_inputs, "chain", pair_all)
    own_part = own_inverse(place, factor)
    other_part = lax.ppermute(own_part, "chain", pair_all)
    half = width // 2
    columns = lax.dynamic_slice_in_dim(scaled_candidates, side * half, half, 1)
    cross = matern(columns, both(archive_inputs, other_archive, 1) * scaling[:, None])
    for_mine, for_yours, solved = join(place, own_part, other_part, cross)

    def hop(value, pairs):
        return lax.ppermute(value, "chain", [(2 * a + i, 2 * b + i) for a, b in pairs for i in range(2)])

    span = 2 * height
    core = lax.axis_index("cand") % 2
    late = after(factor, own_part)

    def send(s):
        chunks = [(late if s else factor)[:, k * span : (k + 1) * span] for k in range(layers)]
        left = jnp.where(odd == 1, chunks[max(2 * s - 1, 0)], chunks[2 * s])
        right = jnp.where(odd == 1, chunks[2 * s], chunks[2 * s + 1])
        mine = jnp.concatenate([left, right], axis=1)
        sent = after(mine, solved) if s else jnp.where(core == 0, left, right)
        got = lax.ppermute(sent, "chain", [(p, p ^ 1) for p in range(chain) if p // 2 >= 2 * s + 1])
        return mine, got

    def share(s, got):
        users = [p for p in range(chain) if p // 2 >= 2 * s + 1]
        twins = [(p * cand + c, p * cand + (c ^ 1)) for p in users for c in range(cand)]
        twin = lax.ppermute(got, ("chain", "cand"), twins)
        return jnp.concatenate(
            [jnp.where(core == 0, got, twin), jnp.where(core == 0, twin, got)], axis=1
        )

    def settle(mine, yours):
        slab = quick(for_mine, mine) + quick(for_yours, yours)
        return after(slab[:, :span]), after(slab[:, span:])

    parts = [send(s) for s in range(layers // 2)]
    slabs = [settle(parts[0][0], share(0, parts[0][1])), settle(*parts[1])]

    far = mid = before = None
    for t in range(layers - 1):
        hops = [(k, t - k, t + 1 + k) for k in range(layers) if t - k >= 0 and t + 1 + k < layers]
        near = hop(solved, [(a, b) for k, a, b in hops if k != 1])
        pairs = [(t - k, t + 2 + k) for k in range(layers) if t - k >= 0 and t + 2 + k < layers]
        if pairs:
            ahead = hop(solved, pairs)
        behind = [(a, b) for k, a, b in hops if k == 1]
        if behind:
            behind = hop(solved, behind)
        users = sorted({t - z // 2 for z in range(t + 1, min(2 * t + 1, layers - 1) + 1)})
        left, right = slabs[users[0]]
        if len(users) > 1:
            second = t - layer // 2 == users[1]
            left = after(jnp.where(second, slabs[users[1]][0], left))
            right = after(jnp.where(second, slabs[users[1]][1], right))
        if mid is not None:
            solved = solved - quick(mid, before, 1)
        if far is not None:
            solved = after(solved - quick(far, left, 1))
        solved = solved - quick(near, right, 1)
        far, mid, before = ahead, (behind if len(behind) else None), right
        if t in (2, 3):
            slabs.append(settle(parts[t][0], after(parts[t][1], solved)))
        if t == 3:
            wanted = jnp.where(unset(solved) == 0, candidate_inputs, 0.0)
    turns = [
        [
            ((2 * z + h) * cand + 8 * k + 2 * x + y, (2 * z + y) * cand + 8 * (h ^ other) + 2 * x + k)
            for z in range(layers)
            for h in range(2)
            for k in range(2)
            for x in range(cand // 4)
            for y in range(2)
        ]
        for other in range(2)
    ]
    turned = []
    for turn in turns:
        turned.append(lax.ppermute(solved, ("chain", "cand"), turn))
    turned = both_of(lax.axis_index("cand") // 8, *turned, 0)
    other_columns = lax.ppermute(solved, "chain", pair_all)
    columns_all = both(solved, other_columns, 0)
    rows = jnp.where(side == 0, columns_all[:, :height], columns_all[:, height:]).T
    twin_columns = lax.ppermute(columns_all, "cand", [(c, c ^ 1) for c in range(cand)])
    others = [turned]
    for r in range(1, cand // 4):
        others.append(lax.ppermute(turned, "cand", [(c, c ^ (2 * r)) for c in range(cand)]))
    others = jnp.concatenate(others, axis=0)
    swap = [(a * cand + b, b * cand + a) for a in range(chain) for b in range(cand)]
    chosen = lax.ppermute(wanted, ("chain", "cand"), swap)
    prior_cov = matern(chosen * after(scaling, solved)[:, None], scaled_candidates)
    theirs = lax.ppermute(quick(others, twin_columns, 1), "cand", [(c, c ^ 1) for c in range(cand)])
    ours = quick(others, columns_all, 1)
    shares = jnp.concatenate([ours, theirs], axis=0).reshape(layers, width, width)
    owners = [
        [(2 * (4 * (c % 2 ^ j) + (c // 2 % 4 ^ r)) + y) * cand + c for j in range(2) for r in range(4)]
        for y in range(2)
        for c in range(cand)
    ]
    shared = lax.all_to_all(
        shares, ("chain", "cand"), 0, 0, axis_index_groups=owners, tiled=True
    ).sum(axis=0)
    return (rows, prior_cov - shared)


def solution(mesh):
    return jax.shard_map(
        shards,
        mesh=mesh,
        in_specs=(P(None, "chain"), P(None, "cand"), P(), P("chain", None)),
        out_specs=(P("chain", "cand"), P("chain", "cand")),
        check_vma=False,
    )
```
